32 devices in a mesh: row: 16 (over z, y, core), col: 2 (over x).
Axes of the slice: x: 2, y: 2, z: 4, core: 2. Of those that a mesh axis runs over, the one named last changes fastest.
Arguments:
- source: float32 [4096, 2048], P('row', 'col'), may hold values from 0.25 to 4
- boxes_a: float32 [16, 8, 512, 512], P('row', 'col'), may hold values from 0.25 to 4
- shifts_a: int32 [16, 8, 2], P('row', 'col'), may hold values from -128 to -1
- widths_a: int32 [16, 8, 2], P('row', 'col'), may hold values from 256 to 512
- boxes_b: float32 [16, 8, 512, 512], P('row', 'col'), may hold values from 0.25 to 4
- shifts_b: int32 [16, 8, 2], P('row', 'col'), may hold values from -128 to -1
- widths_b: int32 [16, 8, 2], P('row', 'col'), may hold values from 256 to 512
Outputs:
- smoothed: float32 [4096, 2048], P('row', 'col')
The draws below stay inside these ranges and needn't reach their ends.
Inputs may be any that keep to these rules, and one draw needn't show every extreme that they name: `shifts_a`: first entry: rows, second: columns. `widths_a`: first entry: rows, second: columns. `shifts_b`: first entry: rows, second: columns. `widths_b`: first entry: rows, second: columns.
All inputs are finite; a program needn't handle non-finite values.
Results may differ from the reference program's by a relative error of at most 0.0003.
Values sent between devices are 32-bit elements; how exact they have to be, the bound alone decides.
A program may use at most 64 MiB of HBM per device.

```python
import math
import jax
import jax.numpy as jnp
from jax import lax

S = 256
BOX = 512
ITERS = 3
RADIUS = 8
CELL_ROWS = 16
CELL_COLS = 8
NR = 4096
NC = 2048


def place_ends(array, stream_key, least, largest):
    index_at = [jax.random.randint(jax.random.fold_in(stream_key, axis), (), 0, length) for axis, length in enumerate(array.shape)]
    widest = array.shape.index(max(array.shape))
    neighbour = index_at[:widest] + [(index_at[widest] + 1) % array.shape[widest]] + index_at[widest + 1:]
    return array.at[tuple(index_at)].set(least).at[tuple(neighbour)].set(largest)


def steps_of(stream_key, extent, pieces, least, largest):
    level, own = 1.0, jax.random.fold_in(stream_key, 6)
    for dim, parts in pieces:
        steps = jnp.exp(jax.random.uniform(jax.random.fold_in(own, dim), (parts,), jnp.float32, least / len(pieces), largest / len(pieces)))
        level = level * jnp.repeat(steps, extent[dim] // parts).reshape([-1 if axis == dim else 1 for axis in range(len(extent))])
    return level


def setup_inputs(seed: int = 0) -> dict:
    arg_keys = jax.random.split(jax.random.key(seed), 8)
    return {
        "source": jnp.clip(jnp.exp(math.log(4.0) - 2.7725887 * jax.random.uniform(arg_keys[0], (NR, NC), jnp.float32) ** steps_of(arg_keys[0], (NR, NC), ((0, 16), (1, 2)), -0.2, 0.2)), 0.25, 4.0),
        "boxes_a": jnp.clip(jnp.exp(math.log(4.0) - 2.7725887 * jax.random.uniform(arg_keys[1], (CELL_ROWS, CELL_COLS, BOX, BOX), jnp.float32) ** steps_of(arg_keys[1], (CELL_ROWS, CELL_COLS, BOX, BOX), ((0, 16), (1, 2)), -0.2, 0.2)), 0.25, 4.0),
        "shifts_a": place_ends(jax.random.randint(arg_keys[2], (CELL_ROWS, CELL_COLS, 2), 0 - S // 2, 0), jax.random.fold_in(arg_keys[2], 1), 0 - S // 2, -1).astype(jnp.int32),
        "widths_a": place_ends(jax.random.randint(arg_keys[3], (CELL_ROWS, CELL_COLS, 2), S, 2 * S + 1), jax.random.fold_in(arg_keys[3], 1), S, 2 * S).astype(jnp.int32),
        "boxes_b": jnp.clip(jnp.exp(math.log(4.0) - 2.7725887 * jax.random.uniform(arg_keys[4], (CELL_ROWS, CELL_COLS, BOX, BOX), jnp.float32) ** steps_of(arg_keys[4], (CELL_ROWS, CELL_COLS, BOX, BOX), ((0, 16), (1, 2)), -0.2, 0.2)), 0.25, 4.0),
        "shifts_b": place_ends(jax.random.randint(arg_keys[5], (CELL_ROWS, CELL_COLS, 2), 0 - S // 2, 0), jax.random.fold_in(arg_keys[5], 1), 0 - S // 2, -1).astype(jnp.int32),
        "widths_b": place_ends(jax.random.randint(arg_keys[6], (CELL_ROWS, CELL_COLS, 2), S, 2 * S + 1), jax.random.fold_in(arg_keys[6], 1), S, 2 * S).astype(jnp.int32),
    }


kernel_eps = 0.05
blur_sigma = 2.0


def table(patch_displacement):
    rows = jnp.arange(S, dtype=jnp.int32)
    cols = jnp.arange(BOX, dtype=jnp.int32)
    dist = (patch_displacement + cols[None, :] - rows[:, None]).astype(jnp.float32) / S
    return jnp.exp(-dist * dist / kernel_eps).astype(jnp.bfloat16)


def masked(patch_rectangle, patch_extent):
    index = jnp.arange(BOX, dtype=jnp.int32)
    keep_rows = (index < patch_extent[0]).astype(jnp.float32)
    keep_cols = (index < patch_extent[1]).astype(jnp.float32)
    return patch_rectangle * keep_rows[:, None] * keep_cols[None, :]


def apply_back(horizontal_kernel_grid, vertical_kernel_grid, multiplier_array):
    inner = jnp.dot(horizontal_kernel_grid.T, multiplier_array.astype(jnp.bfloat16), preferred_element_type=jnp.float32)
    return jnp.dot(inner.astype(jnp.bfloat16), vertical_kernel_grid, preferred_element_type=jnp.float32)


def apply_fwd(horizontal_kernel_grid, vertical_kernel_grid, multiplier_array):
    inner = jnp.dot(horizontal_kernel_grid, multiplier_array.astype(jnp.bfloat16), preferred_element_type=jnp.float32)
    return jnp.dot(inner.astype(jnp.bfloat16), vertical_kernel_grid.T, preferred_element_type=jnp.float32)


def entropic_transport_iterate(probability_measure, patch_rectangle, patch_displacement, patch_extent, initial_corner_index):
    horizontal_kernel_grid = table(patch_displacement[0])
    vertical_kernel_grid = table(patch_displacement[1])
    target = masked(patch_rectangle, patch_extent)
    multiplier_array = initial_corner_index
    lagrange_multiplier_field = target
    for step in range(ITERS):
        lagrange_multiplier_field = target / apply_back(horizontal_kernel_grid, vertical_kernel_grid, multiplier_array)
        multiplier_array = probability_measure / apply_fwd(horizontal_kernel_grid, vertical_kernel_grid, lagrange_multiplier_field)
    return multiplier_array, lagrange_multiplier_field, horizontal_kernel_grid, vertical_kernel_grid


def section_first(probability_measure, patch_rectangle, patch_displacement, patch_extent):
    multiplier_array, lagrange_multiplier_field, horizontal_kernel_grid, vertical_kernel_grid = entropic_transport_iterate(probability_measure, patch_rectangle, patch_displacement, patch_extent, jnp.ones_like(probability_measure))
    return multiplier_array


def section_second(probability_measure, initial_corner_index, patch_rectangle, patch_displacement, patch_extent):
    multiplier_array, lagrange_multiplier_field, horizontal_kernel_grid, vertical_kernel_grid = entropic_transport_iterate(probability_measure, patch_rectangle, patch_displacement, patch_extent, initial_corner_index)
    return lagrange_multiplier_field * apply_back(horizontal_kernel_grid, vertical_kernel_grid, multiplier_array)


def blur_pairs():
    raw = [math.exp(-(step * step) / (2.0 * blur_sigma * blur_sigma)) for step in range(-RADIUS, RADIUS + 1)]
    total = sum(raw)
    return [(step, raw[step + RADIUS] / total) for step in range(-RADIUS, RADIUS + 1)]


def to_cells(field):
    return field.reshape(CELL_ROWS, S, CELL_COLS, S).transpose(0, 2, 1, 3)


def from_cells(cells):
    return cells.transpose(0, 2, 1, 3).reshape(NR, NC)


def reference(source, boxes_a, shifts_a, widths_a, boxes_b, shifts_b, widths_b):
    half = S // 2
    first = lax.map(lambda row: jax.vmap(section_first)(*row), (to_cells(source), boxes_a, shifts_a, widths_a))
    u_first = from_cells(first)
    u_moved = jnp.roll(u_first, (-half, -half), (0, 1))
    mass_moved = jnp.roll(source, (-half, -half), (0, 1))
    plans = lax.map(lambda row: jax.vmap(section_second)(*row),
                    (to_cells(mass_moved), to_cells(u_moved), boxes_b, shifts_b, widths_b))
    canvas = jnp.zeros((NR + 2 * S, NC + 2 * S), jnp.float32)

    def place(index, canvas):
        cell_row = index // CELL_COLS
        cell_col = index % CELL_COLS
        plan = plans[cell_row, cell_col]
        top = (cell_row * S + half + shifts_b[cell_row, cell_col, 0]).astype(jnp.int32)
        left = (cell_col * S + half + shifts_b[cell_row, cell_col, 1]).astype(jnp.int32)
        region = lax.dynamic_slice(canvas, (top, left), (BOX, BOX))
        return lax.dynamic_update_slice(canvas, region + plan, (top, left))

    canvas = lax.fori_loop(0, CELL_ROWS * CELL_COLS, place, canvas)
    folded = canvas[:NR].at[:2 * S].add(canvas[NR:])
    gathered = folded[:, :NC].at[:, :2 * S].add(folded[:, NC:])
    row_smooth = jnp.zeros_like(gathered)
    for step, weight in blur_pairs():
        row_smooth = row_smooth + weight * jnp.roll(gathered, -step, 0)
    smoothed = jnp.zeros_like(gathered)
    for step, weight in blur_pairs():
        smoothed = smoothed + weight * jnp.roll(row_smooth, -step, 1)
    return smoothed
```

```python
import functools
import math

import jax
import jax.numpy as jnp
from jax import lax
from jax.experimental import pallas as pl
from jax.experimental.pallas import tpu as pltpu
from jax.sharding import PartitionSpec as P

S = 256
BOX = 512
ITERS = 3
RADIUS = 8
LANES = 128
HALF = S // 2
DOWN2 = HALF + RADIUS
TALL = RADIUS + 2 * S + DOWN2

kernel_eps = 0.05
blur_sigma = 2.0
blur_total = sum(
    math.exp(-(d * d) / (2.0 * blur_sigma * blur_sigma)) for d in range(-RADIUS, RADIUS + 1)
)


def gauss(offset):
    shape = (LANES, BOX + LANES)
    d = lax.broadcasted_iota(jnp.int32, shape, 1) - lax.broadcasted_iota(jnp.int32, shape, 0)
    g = gauss_of(offset - LANES + d)
    return jnp.concatenate([g[:, LANES:], g[:, :BOX]], axis=0)


def gauss_t(offset):
    shape = (BOX + LANES, LANES)
    d = lax.broadcasted_iota(jnp.int32, shape, 0) - lax.broadcasted_iota(jnp.int32, shape, 1)
    g = gauss_of(offset - LANES + d)
    return jnp.concatenate([g[LANES:], g[:BOX]], axis=1)


def gauss_of(d):
    dist = d.astype(jnp.float32) * (1.0 / S)
    return jnp.exp(dist * dist * (-1.0 / kernel_eps)).astype(jnp.bfloat16)


def blur_weight(d):
    f = d.astype(jnp.float32)
    w = jnp.exp(f * f * (-1.0 / (2.0 * blur_sigma * blur_sigma))) * (1.0 / blur_total)
    return jnp.where(jnp.abs(d) <= RADIUS, w, 0.0)


def split(x):
    hi = x.astype(jnp.bfloat16)
    return hi, (x - hi.astype(jnp.float32)).astype(jnp.bfloat16)


def dot(a, b):
    return jnp.dot(a, b, preferred_element_type=jnp.float32)


def dot_t(a, b):
    return lax.dot_general(a, b, (((1,), (1,)), ((), ())), preferred_element_type=jnp.float32)


def dot_split(a, b):
    (ah, al), (bh, bl) = a, b
    return dot(ah, bh) + (dot(ah, bl) + dot(al, bh))


def bf(x):
    return x.astype(jnp.bfloat16)


def target_of(box_ref, height, width):
    rows = lax.broadcasted_iota(jnp.int32, (BOX, BOX), 0)
    cols = lax.broadcasted_iota(jnp.int32, (BOX, BOX), 1)
    return jnp.where((rows < height) & (cols < width), box_ref[0, 0], 0.0)


MESH = pl.DeviceIdType.MESH
OWN = slice(RADIUS, RADIUS + S)


def tiles(first, count):
    return slice(first * LANES, (first + count) * LANES)


def plan_of(per_dev):
    last = per_dev - 1
    a_order = list(dict.fromkeys([0, last, min(1, last)] + list(range(per_dev - 2, 1, -1))))
    b_order = list(dict.fromkeys([last, 0] + list(range(per_dev - 2, 0, -1))))
    steps = [("a", j) for j in a_order[:3]]
    a_left, b_left = a_order[3:], list(b_order)
    while b_left:
        steps.append(("b", b_left.pop(0)))
        if a_left:
            steps.append(("a", a_left.pop(0)))
    n_tiles = 2 * per_dev + 3
    done, units, sent = [], [], set()
    for g, (kind, j) in enumerate(steps):
        if kind == "a":
            continue
        done.append(j)
        ready = [
            t
            for t in range(n_tiles)
            if t not in sent
            and all(i in done for i in range(per_dev) if 2 * i <= t <= 2 * i + 4)
        ]
        sent.update(ready)
        runs = []
        for t in reversed(ready):
            if runs and runs[-1][0] == t + 1 and runs[-1][1] < 3:
                runs[-1] = (t, runs[-1][1] + 1)
            else:
                runs.append((t, 1))
        units += [(g, first, count) for first, count in runs]
    return steps, units


def kernel(
    per_dev,
    n_row,
    n_col,
    shifts_a,
    widths_a,
    shifts_b,
    widths_b,
    src,
    box_a,
    box_b,
    out,
    tgt,
    u_loc,
    mv_s,
    mv_u,
    canvas,
    band_hi,
    band_lo,
    r1,
    r2,
    rup,
    sb,
    cs,
    cl,
    s_send,
    s_recv,
    u_send,
    u_recv,
    x_send,
    x_recv,
    c_send,
    c_recv,
):
    g = pl.program_id(0)
    cols = per_dev * S
    n_tiles = 2 * per_dev + 3
    row, col = lax.axis_index("row"), lax.axis_index("col")
    odd = lax.rem(row, 2) == 1
    even = lax.rem(row, 2) == 0
    steps, units = plan_of(per_dev)
    n_steps = len(steps)

    def pick(values):
        res = jnp.int32(values[0])
        for k in range(1, n_steps):
            res = jnp.where(g == k, jnp.int32(values[k]), res)
        return res

    j = pick([c for _, c in steps])
    is_a = pick([int(k == "a") for k, _ in steps]) == 1

    def at(dr, dc):
        return (lax.rem(row + dr + n_row, n_row), lax.rem(col + dc + n_col, n_col))

    def remote(a, b, send, recv, to):
        return pltpu.make_async_remote_copy(
            src_ref=a, dst_ref=b, send_sem=send, recv_sem=recv, device_id=to, device_id_type=MESH
        )

    upper, lower = slice(0, HALF), slice(HALF, S)
    edge = slice(cols - LANES, cols)

    def halo(field, moved, k, send, recv):
        if k == 0:
            a, b, to = field.at[upper, HALF:], moved.at[lower, : cols - HALF], at(-1, 0)
        elif k == 1:
            a, b, to = field.at[upper, :LANES], moved.at[lower, edge], at(-1, -1)
        else:
            a, b, to = field.at[lower, :LANES], moved.at[upper, edge], at(0, -1)
        return remote(a, b, send.at[k], recv.at[k], to)

    def chunk(j):
        lo, hi = max(j * S, HALF), (j + 1) * S
        return remote(
            u_loc.at[upper, lo:hi],
            mv_u.at[lower, lo - HALF : hi - HALF],
            u_send.at[2 + j],
            u_recv.at[2 + j],
            at(-1, 0),
        )

    def corner(k):
        a = u_loc.at[upper, :LANES] if k == 0 else u_loc.at[lower, :LANES]
        b = mv_u.at[lower, edge] if k == 0 else mv_u.at[upper, edge]
        return remote(a, b, u_send.at[k], u_recv.at[k], at(-1, -1) if k == 0 else at(0, -1))

    near, far = RADIUS + S, RADIUS + 2 * S
    mid = near + DOWN2

    def spill(n, kind):
        _, first, count = units[n]
        c = tiles(first, count)
        a, b, to, k = {
            "even_far": (canvas.at[far:, c], r1.at[S:, c], at(1, 0), 0),
            "even_near": (canvas.at[near:far, c], r1.at[:S, c], at(1, 0), 1),
            "odd_near": (canvas.at[near:mid, c], r1.at[:DOWN2, c], at(1, 0), 0),
            "odd_mid": (canvas.at[mid:far, c], r1.at[DOWN2:S, c], at(1, 0), 1),
            "odd_far": (canvas.at[far:, c], r2.at[:, c], at(2, 0), 2),
            "up": (canvas.at[:RADIUS, c], rup.at[:, c], at(-1, 0), 3),
        }[kind]
        return remote(a, b, x_send.at[n, k], x_recv.at[n, k], to)

    flank = slice(0, 3 * LANES)
    tip = slice(3 * LANES, 4 * LANES)

    def beside(k):
        if k == 0:
            a, b, to = sb.at[:, flank], cs.at[:, flank], at(0, 1)
        elif k == 1:
            a, b, to = sb.at[:, tip], cs.at[:, tip], at(0, 1)
        else:
            a, b, to = sb.at[:, tip], cl, at(0, -1)
        return remote(a, b, c_send.at[k], c_recv.at[k], to)

    sides = 2 if n_col == 2 else 3

    def give(n):
        @pl.when(even)
        def _():
            spill(n, "even_far").start()
            spill(n, "even_near").start()

        @pl.when(odd)
        def _():
            spill(n, "odd_far").start()
            spill(n, "odd_mid").start()

        spill(n, "up").start()

    def hand_on(n):
        @pl.when(odd)
        def _():
            c = tiles(units[n][1], units[n][2])
            spill(n, "even_far").wait_recv()
            canvas[near:mid, c] += r1[S:, c]
            spill(n, "odd_near").start()

    def between():
        for k in range(1, n_steps):
            ready = [n for n, u in enumerate(units) if u[0] == k - 1]
            if ready:

                @pl.when(g == k)
                def _():
                    for n in ready:
                        hand_on(n)

    def fold(n):
        c = tiles(units[n][1], units[n][2])

        @pl.when(even)
        def _():
            spill(n, "odd_near").wait_recv()
            spill(n, "odd_mid").wait_recv()
            canvas[OWN, c] += r1[:S, c]

        @pl.when(odd)
        def _():
            spill(n, "even_near").wait_recv()
            spill(n, "odd_far").wait_recv()
            canvas[OWN, c] += r1[:S, c]
            canvas[RADIUS : RADIUS + DOWN2, c] += r2[:, c]

        spill(n, "up").wait_recv()
        canvas[S : RADIUS + S, c] += rup[:, c]

    def smooth(first, count):
        lo, hi = max(first - 1, 0), min(first + count + 1, n_tiles)
        rows = slice((lo - first + 1) * LANES, (hi - first + 1) * LANES)
        field = split(canvas[OWN, lo * LANES : hi * LANES])
        return dot_split(field, [b[rows, : count * LANES] for b in (band_hi, band_lo)])

    def the_band():
        n = lax.broadcasted_iota(jnp.int32, (2 * S, S), 0)
        m = lax.broadcasted_iota(jnp.int32, (2 * S, S), 1)
        return split(blur_weight(n - LANES - m))

    @pl.when(is_a)
    def _():
        barrier = pltpu.get_barrier_semaphore()
        peers = [(-1, 0), (1, 0), (-2, 0), (2, 0), (0, -1), (0, 1), (-1, -1), (1, 1)]

        @pl.when(g == 0)
        def _():
            for dr, dc in peers:
                pl.semaphore_signal(barrier, inc=1, device_id=at(dr, dc), device_id_type=MESH)
            mv_s[upper, : cols - HALF] = src[lower, HALF:]
            canvas[...] = jnp.zeros_like(canvas)
            band_hi[...], band_lo[...] = the_band()

        o_r, o_c = shifts_a[0, 0, j], shifts_a[0, 1, j]
        h, w = widths_a[0, 0, j], widths_a[0, 1, j]
        kr = gauss(o_r)
        krt = gauss_t(o_r)
        kc = gauss(o_c)
        tgt[...] = target_of(box_a, h, w)
        here = pl.ds(pl.multiple_of(j * S, S), S)
        a = src[:, here]
        in_r = bf(jnp.sum(krt.astype(jnp.float32), axis=1, keepdims=True)).astype(jnp.float32)
        in_c = jnp.sum(kc.astype(jnp.float32), axis=0, keepdims=True)
        back = in_r * in_c
        for step in range(ITERS):
            v = bf(tgt[...] / back)
            u = a / dot_t(bf(dot(kr, v)), kc)
            if step < ITERS - 1:
                back = dot(bf(dot(krt, bf(u))), kc)
            if step == 0:

                @pl.when(g == 0)
                def _():
                    pl.semaphore_wait(barrier, len(peers))
                    for k in range(3):
                        halo(src, mv_s, k, s_send, s_recv).start()

                between()
        u_loc[:, here] = u

        @pl.when(g == 0)
        def _():
            for k in range(2):
                corner(k).start()

        for i in range(per_dev):

            @pl.when(j == i)
            def _():
                chunk(i).start()
                lo, hi = max(i * S, HALF), (i + 1) * S
                mv_u[upper, lo - HALF : hi - HALF] = u_loc[lower, lo:hi]

    @pl.when(jnp.logical_not(is_a))
    def _():
        waited = set()
        for k, (kind, i) in enumerate(steps):
            if kind == "a":
                continue
            need = [c for c in (i, i + 1) if c < per_dev and c not in waited]
            waited.update(need)

            @pl.when(g == k)
            def _():
                if len(waited) == len(need):
                    halo(src, mv_s, 0, s_send, s_recv).wait_recv()
                if i == per_dev - 1:
                    for c in range(1, 3):
                        halo(src, mv_s, c, s_send, s_recv).wait_recv()
                    for c in range(2):
                        corner(c).wait_recv()
                for c in need:
                    chunk(c).wait_recv()

        o_r, o_c = shifts_b[0, 0, j], shifts_b[0, 1, j]
        h, w = widths_b[0, 0, j], widths_b[0, 1, j]
        kr = gauss(o_r)
        krt = gauss_t(o_r)
        kc = gauss(o_c)
        tgt[...] = target_of(box_b, h, w)
        here = pl.ds(pl.multiple_of(j * S, S), S)
        a = mv_s[:, here]
        u = mv_u[:, here]
        for step in range(ITERS):
            back = dot(bf(dot(krt, bf(u))), kc)
            v = tgt[...] / back
            u = a / dot_t(bf(dot(kr, bf(v))), kc)
            if step == 0:
                between()

        plan = v * dot(bf(dot(krt, bf(u))), kc)

        r = lax.broadcasted_iota(jnp.int32, (LANES, 3 * LANES), 0) - RADIUS
        m = lax.broadcasted_iota(jnp.int32, (LANES, 3 * LANES), 1) - 2 * LANES
        weights = split(blur_weight(HALF + o_r + m - r))
        halves = split(plan)
        parts = []
        for b in range(-(-TALL // LANES)):
            height = min(LANES, TALL - b * LANES)
            lo, hi = max(b - 2, 0), min(b + 1, BOX // LANES)
            wt = slice((lo - b + 2) * LANES, (hi - b + 2) * LANES)
            parts.append(
                dot_split(
                    [x[:height, wt] for x in weights],
                    [x[lo * LANES : hi * LANES] for x in halves],
                )
            )
        rowed = jnp.concatenate(parts, axis=0)
        s = HALF + o_c
        lane = lax.broadcasted_iota(jnp.int32, (TALL, LANES), 1)
        turned = [pltpu.roll(rowed[:, tiles(t, 1)], s, 1) for t in range(BOX // LANES)]
        zero = jnp.zeros((TALL, LANES), jnp.float32)
        for t in range(BOX // LANES + 1):
            left = turned[t - 1] if t > 0 else zero
            right = turned[t] if t < BOX // LANES else zero
            spot = pl.ds(pl.multiple_of(j * S + t * LANES, LANES), LANES)
            canvas[:, spot] += jnp.where(lane < s, left, right)

        for k in range(n_steps):
            ready = [n for n, u_ in enumerate(units) if u_[0] == k]
            if ready:

                @pl.when(g == k)
                def _():
                    for n in ready:
                        give(n)

        @pl.when(g == n_steps - 1)
        def _():
            final = [n for n, u_ in enumerate(units) if u_[0] == n_steps - 1]
            early = [n for n in range(len(units)) if n not in final]
            fold(early[0])
            for n in final:
                hand_on(n)
            for n in early[1:]:
                fold(n)

            first = 2 * per_dev
            sb[:, 2 * LANES : 3 * LANES] = smooth(first + 2, 1)
            sb[:, : 2 * LANES] = smooth(first, 2)
            over = split(canvas[OWN, tiles(n_tiles - 1, 1)])
            under = split(canvas[OWN, tiles(0, 1)])
            sb[:, tip] = dot_split(over, [b[:LANES, :LANES] for b in (band_hi, band_lo)]) + dot_split(
                under, [b[2 * LANES : 3 * LANES, :LANES] for b in (band_hi, band_lo)]
            )
            for k in range(sides):
                beside(k).start()

            ready = set()
            for n in early:
                ready.update(range(units[n][1], units[n][1] + units[n][2]))
            shown = set()

            def show():
                t = 2 * per_dev - 1
                while t >= 0:
                    ok = lambda x: x not in shown and all(
                        y in ready for y in (x - 1, x, x + 1) if 0 <= y < n_tiles
                    )
                    if ok(t):
                        count = 2 if t > 0 and ok(t - 1) else 1
                        base = t - count + 1
                        out[:, tiles(base, count)] = smooth(base, count)
                        shown.update(range(base, t + 1))
                        t -= count
                    else:
                        t -= 1

            show()
            for n in final:
                fold(n)
                ready.update(range(units[n][1], units[n][1] + units[n][2]))
                show()

            ln = lax.broadcasted_iota(jnp.int32, (S, LANES), 1)
            for k in range(sides):
                beside(k).wait_recv()
            out[:, flank] += cs[:, flank]
            out[:, tip] += jnp.where(ln < LANES - RADIUS, cs[:, tip], 0.0)
            behind = cs[:, tip] if n_col == 2 else cl[...]
            out[:, edge] += jnp.where(ln >= LANES - RADIUS, behind, 0.0)

            for k in range(3):
                halo(src, mv_s, k, s_send, s_recv).wait_send()
            for k in range(2):
                corner(k).wait_send()
            for i in range(per_dev):
                chunk(i).wait_send()
            for k in range(sides):
                beside(k).wait_send()
            for n in range(len(units)):
                spill(n, "up").wait_send()

                @pl.when(even)
                def _():
                    spill(n, "even_far").wait_send()
                    spill(n, "even_near").wait_send()

                @pl.when(odd)
                def _():
                    spill(n, "odd_near").wait_send()
                    spill(n, "odd_mid").wait_send()
                    spill(n, "odd_far").wait_send()


def on_device(n_row, n_col, source, boxes_a, shifts_a, widths_a, boxes_b, shifts_b, widths_b):
    cols = source.shape[1]
    per_dev = cols // S
    wide = cols + 3 * LANES
    steps, units = plan_of(per_dev)
    f32 = lambda *shape: pltpu.VMEM(shape, jnp.float32)
    dma = pltpu.SemaphoreType.DMA
    box = (1, 1, BOX, BOX)

    def boxes_of(kind):
        def where(g):
            block = None
            for k in range(len(steps) - 1, -1, -1):
                if steps[k][0] != kind:
                    continue
                block = jnp.int32(steps[k][1]) if block is None else jnp.where(g <= k, steps[k][1], block)
            return (0, block, 0, 0)

        return pl.BlockSpec(box, where)

    smem = pl.BlockSpec(memory_space=pltpu.SMEM)
    return pl.pallas_call(
        functools.partial(kernel, per_dev, n_row, n_col),
        grid_spec=pltpu.PrefetchScalarGridSpec(
            num_scalar_prefetch=0,
            grid=(len(steps),),
            in_specs=[
                smem,
                smem,
                smem,
                smem,
                pl.BlockSpec((S, cols), lambda g: (0, 0)),
                boxes_of("a"),
                boxes_of("b"),
            ],
            out_specs=pl.BlockSpec((S, cols), lambda g: (0, 0)),
            scratch_shapes=[
                f32(BOX, BOX),
                f32(S, cols),
                f32(S, cols),
                f32(S, cols),
                f32(TALL, wide),
                pltpu.VMEM((2 * S, S), jnp.bfloat16),
                pltpu.VMEM((2 * S, S), jnp.bfloat16),
                f32(S + DOWN2, wide),
                f32(DOWN2, wide),
                f32(RADIUS, wide),
                f32(S, 4 * LANES),
                f32(S, 4 * LANES),
                f32(S, LANES),
                dma((3,)),
                dma((3,)),
                dma((2 + per_dev,)),
                dma((2 + per_dev,)),
                dma((len(units), 4)),
                dma((len(units), 4)),
                dma((3,)),
                dma((3,)),
            ],
        ),
        out_shape=jax.ShapeDtypeStruct((S, cols), jnp.float32),
        compiler_params=pltpu.CompilerParams(
            vmem_limit_bytes=56 * 1024 * 1024, collective_id=0, has_side_effects=True
        ),
        name="transport",
    )(*[x.swapaxes(1, 2) for x in (shifts_a, widths_a, shifts_b, widths_b)], source, boxes_a, boxes_b)


def solution(mesh):
    return jax.shard_map(
        functools.partial(on_device, mesh.shape["row"], mesh.shape["col"]),
        mesh=mesh,
        in_specs=(
            P("row", "col"),
            P("row", "col", None, None),
            P("row", "col", None),
            P("row", "col", None),
            P("row", "col", None, None),
            P("row", "col", None),
            P("row", "col", None),
        ),
        out_specs=P("row", "col"),
        check_vma=False,
    )
```

```python
import functools
import math

import jax
import jax.numpy as jnp
from jax import lax
from jax.experimental import pallas as pl
from jax.experimental.pallas import tpu as pltpu
from jax.sharding import PartitionSpec as P

S = 256
BOX = 512
ITERS = 3
RADIUS = 8
LANES = 128
HALF = S // 2
DOWN2 = HALF + RADIUS
TALL = RADIUS + 2 * S + DOWN2

kernel_eps = 0.05
blur_sigma = 2.0
blur_total = sum(
    math.exp(-(d * d) / (2.0 * blur_sigma * blur_sigma)) for d in range(-RADIUS, RADIUS + 1)
)


def gauss(offset):
    shape = (LANES, BOX + LANES)
    d = lax.broadcasted_iota(jnp.int32, shape, 1) - lax.broadcasted_iota(jnp.int32, shape, 0)
    g = gauss_of(offset - LANES + d)
    return jnp.concatenate([g[:, LANES:], g[:, :BOX]], axis=0)


def gauss_t(offset):
    shape = (BOX + LANES, LANES)
    d = lax.broadcasted_iota(jnp.int32, shape, 0) - lax.broadcasted_iota(jnp.int32, shape, 1)
    g = gauss_of(offset - LANES + d)
    return jnp.concatenate([g[LANES:], g[:BOX]], axis=1)


def gauss_of(d):
    dist = d.astype(jnp.float32) * (1.0 / S)
    return jnp.exp(dist * dist * (-1.0 / kernel_eps)).astype(jnp.bfloat16)


def blur_weight(d):
    f = d.astype(jnp.float32)
    w = jnp.exp(f * f * (-1.0 / (2.0 * blur_sigma * blur_sigma))) * (1.0 / blur_total)
    return jnp.where(jnp.abs(d) <= RADIUS, w, 0.0)


def split(x):
    hi = x.astype(jnp.bfloat16)
    return hi, (x - hi.astype(jnp.float32)).astype(jnp.bfloat16)


def dot(a, b):
    return jnp.dot(a, b, preferred_element_type=jnp.float32)


def dot_t(a, b):
    return lax.dot_general(a, b, (((1,), (1,)), ((), ())), preferred_element_type=jnp.float32)


def dot_split(a, b):
    (ah, al), (bh, bl) = a, b
    return dot(ah, bh) + (dot(ah, bl) + dot(al, bh))


def bf(x):
    return x.astype(jnp.bfloat16)


def target_of(box_ref, height, width):
    rows = lax.broadcasted_iota(jnp.int32, (BOX, BOX), 0)
    cols = lax.broadcasted_iota(jnp.int32, (BOX, BOX), 1)
    return jnp.where((rows < height) & (cols < width), box_ref[0, 0], 0.0)


MESH = pl.DeviceIdType.MESH
OWN = slice(RADIUS, RADIUS + S)


def tiles(first, count):
    return slice(first * LANES, (first + count) * LANES)


def plan_of(per_dev):
    last = per_dev - 1
    a_order = list(dict.fromkeys([0, last, min(1, last)] + list(range(per_dev - 2, 1, -1))))
    b_order = list(dict.fromkeys([last, 0] + list(range(per_dev - 2, 0, -1))))
    steps = [("a", tuple(a_order[k : k + 2])) for k in range(0, per_dev, 2)]
    steps += [("b", (j,)) for j in b_order]
    n_tiles = 2 * per_dev + 3
    done, units, sent = [], [], set()
    for g, (kind, cells) in enumerate(steps):
        if kind == "a":
            continue
        done += cells
        ready = [
            t
            for t in range(n_tiles)
            if t not in sent
            and all(i in done for i in range(per_dev) if 2 * i <= t <= 2 * i + 4)
        ]
        sent.update(ready)
        runs = []
        for t in reversed(ready):
            if runs and runs[-1][0] == t + 1 and runs[-1][1] < 3:
                runs[-1] = (t, runs[-1][1] + 1)
            else:
                runs.append((t, 1))
        units += [(g, first, count) for first, count in runs]
    return steps, units


def kernel(
    per_dev,
    n_row,
    n_col,
    shifts_a,
    widths_a,
    shifts_b,
    widths_b,
    src,
    box_a,
    box_c,
    box_b,
    out,
    tgt,
    tgt_c,
    u_loc,
    mv_s,
    mv_u,
    canvas,
    band_hi,
    band_lo,
    r1,
    r2,
    rup,
    sb,
    cs,
    cl,
    s_send,
    s_recv,
    u_send,
    u_recv,
    x_send,
    x_recv,
    c_send,
    c_recv,
):
    g = pl.program_id(0)
    cols = per_dev * S
    n_tiles = 2 * per_dev + 3
    row, col = lax.axis_index("row"), lax.axis_index("col")
    odd = lax.rem(row, 2) == 1
    even = lax.rem(row, 2) == 0
    steps, units = plan_of(per_dev)
    n_steps = len(steps)

    def pick(values):
        res = jnp.int32(values[0])
        for k in range(1, n_steps):
            res = jnp.where(g == k, jnp.int32(values[k]), res)
        return res

    j, j_c = pick([c[0] for _, c in steps]), pick([c[-1] for _, c in steps])
    is_a = pick([int(k == "a") for k, _ in steps]) == 1

    def at(dr, dc):
        return (lax.rem(row + dr + n_row, n_row), lax.rem(col + dc + n_col, n_col))

    def remote(a, b, send, recv, to):
        return pltpu.make_async_remote_copy(
            src_ref=a, dst_ref=b, send_sem=send, recv_sem=recv, device_id=to, device_id_type=MESH
        )

    upper, lower = slice(0, HALF), slice(HALF, S)
    edge = slice(cols - LANES, cols)

    def halo(field, moved, k, send, recv):
        if k == 0:
            a, b, to = field.at[upper, :LANES], moved.at[lower, edge], at(-1, -1)
        elif k == 1:
            a, b, to = field.at[lower, :LANES], moved.at[upper, edge], at(0, -1)
        else:
            lo, hi = max((k - 2) * S, HALF), (k - 1) * S
            a, b, to = field.at[upper, lo:hi], moved.at[lower, lo - HALF : hi - HALF], at(-1, 0)
        return remote(a, b, send.at[k], recv.at[k], to)

    def mass(k):
        return halo(src, mv_s, k, s_send, s_recv)

    def scale(k):
        return halo(u_loc, mv_u, k, u_send, u_recv)

    near, far = RADIUS + S, RADIUS + 2 * S
    mid = near + DOWN2

    def spill(n, kind):
        _, first, count = units[n]
        c = tiles(first, count)
        a, b, to, k = {
            "even_far": (canvas.at[far:, c], r1.at[S:, c], at(1, 0), 0),
            "even_near": (canvas.at[near:far, c], r1.at[:S, c], at(1, 0), 1),
            "odd_near": (canvas.at[near:mid, c], r1.at[:DOWN2, c], at(1, 0), 0),
            "odd_mid": (canvas.at[mid:far, c], r1.at[DOWN2:S, c], at(1, 0), 1),
            "odd_far": (canvas.at[far:, c], r2.at[:, c], at(2, 0), 2),
            "up": (canvas.at[:RADIUS, c], rup.at[:, c], at(-1, 0), 3),
        }[kind]
        return remote(a, b, x_send.at[n, k], x_recv.at[n, k], to)

    flank = slice(0, 3 * LANES)
    tip = slice(3 * LANES, 4 * LANES)

    def beside(k):
        if k == 0:
            a, b, to = sb.at[:, flank], cs.at[:, flank], at(0, 1)
        elif k == 1:
            a, b, to = sb.at[:, tip], cs.at[:, tip], at(0, 1)
        else:
            a, b, to = sb.at[:, tip], cl, at(0, -1)
        return remote(a, b, c_send.at[k], c_recv.at[k], to)

    sides = 2 if n_col == 2 else 3

    def give(n):
        @pl.when(even)
        def _():
            spill(n, "even_far").start()
            spill(n, "even_near").start()

        @pl.when(odd)
        def _():
            spill(n, "odd_far").start()
            spill(n, "odd_mid").start()

        spill(n, "up").start()

    def hand_on(n):
        @pl.when(odd)
        def _():
            c = tiles(units[n][1], units[n][2])
            spill(n, "even_far").wait_recv()
            canvas[near:mid, c] += r1[S:, c]
            spill(n, "odd_near").start()

    def between():
        for k in range(1, n_steps):
            ready = [n for n, u in enumerate(units) if u[0] == k - 1]
            if ready:

                @pl.when(g == k)
                def _():
                    for n in ready:
                        hand_on(n)

    def fold(n):
        c = tiles(units[n][1], units[n][2])

        @pl.when(even)
        def _():
            spill(n, "odd_near").wait_recv()
            spill(n, "odd_mid").wait_recv()
            canvas[OWN, c] += r1[:S, c]

        @pl.when(odd)
        def _():
            spill(n, "even_near").wait_recv()
            spill(n, "odd_far").wait_recv()
            canvas[OWN, c] += r1[:S, c]
            canvas[RADIUS : RADIUS + DOWN2, c] += r2[:, c]

        spill(n, "up").wait_recv()
        canvas[S : RADIUS + S, c] += rup[:, c]

    def smooth(first, count):
        lo, hi = max(first - 1, 0), min(first + count + 1, n_tiles)
        rows = slice((lo - first + 1) * LANES, (hi - first + 1) * LANES)
        field = split(canvas[OWN, lo * LANES : hi * LANES])
        return dot_split(field, [b[rows, : count * LANES] for b in (band_hi, band_lo)])

    def the_band():
        n = lax.broadcasted_iota(jnp.int32, (2 * S, S), 0)
        m = lax.broadcasted_iota(jnp.int32, (2 * S, S), 1)
        return split(blur_weight(n - LANES - m))

    @pl.when(is_a)
    def _():
        barrier = pltpu.get_barrier_semaphore()
        peers = [(-1, 0), (1, 0), (-2, 0), (2, 0), (0, -1), (0, 1), (-1, -1), (1, 1)]

        @pl.when(g == 0)
        def _():
            for dr, dc in peers:
                pl.semaphore_signal(barrier, inc=1, device_id=at(dr, dc), device_id_type=MESH)
            mv_s[upper, : cols - HALF] = src[lower, HALF:]
            canvas[...] = jnp.zeros_like(canvas)
            band_hi[...], band_lo[...] = the_band()

        cells = []
        for c, box, t in ((j, box_a, tgt), (j_c, box_c, tgt_c)):
            o_r, o_c = shifts_a[0, 0, c], shifts_a[0, 1, c]
            h, w = widths_a[0, 0, c], widths_a[0, 1, c]
            krt, kc = gauss_t(o_r), gauss(o_c)
            t[...] = target_of(box, h, w)
            here = pl.ds(pl.multiple_of(c * S, S), S)
            in_r = bf(jnp.sum(krt.astype(jnp.float32), axis=1, keepdims=True)).astype(jnp.float32)
            in_c = jnp.sum(kc.astype(jnp.float32), axis=0, keepdims=True)
            cells.append((gauss(o_r), krt, kc, t, src[:, here], here, in_r * in_c))
        back = [c[-1] for c in cells]
        for step in range(ITERS):
            v = [bf(c[3][...] / b) for c, b in zip(cells, back)]
            inner = [bf(dot(c[0], x)) for c, x in zip(cells, v)]
            u = [c[4] / dot_t(x, c[2]) for c, x in zip(cells, inner)]
            if step < ITERS - 1:
                inner = [bf(dot(c[1], bf(x))) for c, x in zip(cells, u)]
                back = [dot(x, c[2]) for c, x in zip(cells, inner)]
            if step == 0:

                @pl.when(g == 0)
                def _():
                    pl.semaphore_wait(barrier, len(peers))
                    for k in (0, 1, 1 + per_dev, 2):
                        mass(k).start()

        for c, x in zip(cells, u):
            u_loc[:, c[5]] = x

        for n, (kind, pair) in enumerate(steps):
            if kind == "b":
                continue

            @pl.when(g == n)
            def _():
                if n == 0:
                    scale(0).start()
                    scale(1).start()
                for i in reversed(pair):
                    scale(2 + i).start()
                if n == 0:
                    for k in range(per_dev, 2, -1):
                        mass(k).start()
                for i in pair:
                    lo, hi = max(i * S, HALF), (i + 1) * S
                    mv_u[upper, lo - HALF : hi - HALF] = u_loc[lower, lo:hi]

    @pl.when(jnp.logical_not(is_a))
    def _():
        waited = set()
        for k, (kind, pair) in enumerate(steps):
            if kind == "a":
                continue
            (i,) = pair
            need = [2 + c for c in (i, i + 1) if c < per_dev]
            need = [c for c in need + [0, 1] * (i == per_dev - 1) if c not in waited]
            waited.update(need)

            @pl.when(g == k)
            def _():
                for c in need:
                    mass(c).wait_recv()
                    scale(c).wait_recv()

        o_r, o_c = shifts_b[0, 0, j], shifts_b[0, 1, j]
        h, w = widths_b[0, 0, j], widths_b[0, 1, j]
        kr = gauss(o_r)
        krt = gauss_t(o_r)
        kc = gauss(o_c)
        tgt[...] = target_of(box_b, h, w)
        here = pl.ds(pl.multiple_of(j * S, S), S)
        a = mv_s[:, here]
        u = mv_u[:, here]
        for step in range(ITERS):
            back = dot(bf(dot(krt, bf(u))), kc)
            v = tgt[...] / back
            u = a / dot_t(bf(dot(kr, bf(v))), kc)
            if step == 0:
                between()

        plan = v * dot(bf(dot(krt, bf(u))), kc)

        r = lax.broadcasted_iota(jnp.int32, (LANES, 3 * LANES), 0) - RADIUS
        m = lax.broadcasted_iota(jnp.int32, (LANES, 3 * LANES), 1) - 2 * LANES
        weights = split(blur_weight(HALF + o_r + m - r))
        halves = split(plan)
        parts = []
        for b in range(-(-TALL // LANES)):
            height = min(LANES, TALL - b * LANES)
            lo, hi = max(b - 2, 0), min(b + 1, BOX // LANES)
            wt = slice((lo - b + 2) * LANES, (hi - b + 2) * LANES)
            parts.append(
                dot_split(
                    [x[:height, wt] for x in weights],
                    [x[lo * LANES : hi * LANES] for x in halves],
                )
            )
        rowed = jnp.concatenate(parts, axis=0)
        s = HALF + o_c
        lane = lax.broadcasted_iota(jnp.int32, (TALL, LANES), 1)
        turned = [pltpu.roll(rowed[:, tiles(t, 1)], s, 1) for t in range(BOX // LANES)]
        zero = jnp.zeros((TALL, LANES), jnp.float32)
        for t in range(BOX // LANES + 1):
            left = turned[t - 1] if t > 0 else zero
            right = turned[t] if t < BOX // LANES else zero
            spot = pl.ds(pl.multiple_of(j * S + t * LANES, LANES), LANES)
            canvas[:, spot] += jnp.where(lane < s, left, right)

        for k in range(n_steps):
            ready = [n for n, u_ in enumerate(units) if u_[0] == k]
            if ready:

                @pl.when(g == k)
                def _():
                    for n in ready:
                        give(n)

        @pl.when(g == n_steps - 1)
        def _():
            final = [n for n, u_ in enumerate(units) if u_[0] == n_steps - 1]
            early = [n for n in range(len(units)) if n not in final]
            fold(early[0])
            for n in final:
                hand_on(n)
            for n in early[1:]:
                fold(n)

            first = 2 * per_dev
            sb[:, 2 * LANES : 3 * LANES] = smooth(first + 2, 1)
            sb[:, : 2 * LANES] = smooth(first, 2)
            over = split(canvas[OWN, tiles(n_tiles - 1, 1)])
            under = split(canvas[OWN, tiles(0, 1)])
            sb[:, tip] = dot_split(over, [b[:LANES, :LANES] for b in (band_hi, band_lo)]) + dot_split(
                under, [b[2 * LANES : 3 * LANES, :LANES] for b in (band_hi, band_lo)]
            )
            for k in range(sides):
                beside(k).start()

            ready = set()
            for n in early:
                ready.update(range(units[n][1], units[n][1] + units[n][2]))
            shown = set()

            def show():
                t = 2 * per_dev - 1
                while t >= 0:
                    ok = lambda x: x not in shown and all(
                        y in ready for y in (x - 1, x, x + 1) if 0 <= y < n_tiles
                    )
                    if ok(t):
                        count = 2 if t > 0 and ok(t - 1) else 1
                        base = t - count + 1
                        out[:, tiles(base, count)] = smooth(base, count)
                        shown.update(range(base, t + 1))
                        t -= count
                    else:
                        t -= 1

            show()
            for n in final:
                fold(n)
                ready.update(range(units[n][1], units[n][1] + units[n][2]))
                show()

            ln = lax.broadcasted_iota(jnp.int32, (S, LANES), 1)
            for k in range(sides):
                beside(k).wait_recv()
            out[:, flank] += cs[:, flank]
            out[:, tip] += jnp.where(ln < LANES - RADIUS, cs[:, tip], 0.0)
            behind = cs[:, tip] if n_col == 2 else cl[...]
            out[:, edge] += jnp.where(ln >= LANES - RADIUS, behind, 0.0)

            for k in range(2 + per_dev):
                mass(k).wait_send()
                scale(k).wait_send()
            for k in range(sides):
                beside(k).wait_send()
            for n in range(len(units)):
                spill(n, "up").wait_send()

                @pl.when(even)
                def _():
                    spill(n, "even_far").wait_send()
                    spill(n, "even_near").wait_send()

                @pl.when(odd)
                def _():
                    spill(n, "odd_near").wait_send()
                    spill(n, "odd_mid").wait_send()
                    spill(n, "odd_far").wait_send()


def on_device(n_row, n_col, source, boxes_a, shifts_a, widths_a, boxes_b, shifts_b, widths_b):
    cols = source.shape[1]
    per_dev = cols // S
    wide = cols + 3 * LANES
    steps, units = plan_of(per_dev)
    f32 = lambda *shape: pltpu.VMEM(shape, jnp.float32)
    dma = pltpu.SemaphoreType.DMA
    box = (1, 1, BOX, BOX)

    def boxes_of(kind, side):
        def where(g):
            block = None
            for k in range(len(steps) - 1, -1, -1):
                if steps[k][0] != kind:
                    continue
                cell = steps[k][1][side]
                block = jnp.int32(cell) if block is None else jnp.where(g <= k, cell, block)
            return (0, block, 0, 0)

        return pl.BlockSpec(box, where)

    smem = pl.BlockSpec(memory_space=pltpu.SMEM)
    return pl.pallas_call(
        functools.partial(kernel, per_dev, n_row, n_col),
        grid_spec=pltpu.PrefetchScalarGridSpec(
            num_scalar_prefetch=0,
            grid=(len(steps),),
            in_specs=[
                smem,
                smem,
                smem,
                smem,
                pl.BlockSpec((S, cols), lambda g: (0, 0)),
                boxes_of("a", 0),
                boxes_of("a", -1),
                boxes_of("b", 0),
            ],
            out_specs=pl.BlockSpec(memory_space=pltpu.VMEM),
            scratch_shapes=[
                f32(BOX, BOX),
                f32(BOX, BOX),
                f32(S, cols),
                f32(S, cols),
                f32(S, cols),
                f32(TALL, wide),
                pltpu.VMEM((2 * S, S), jnp.bfloat16),
                pltpu.VMEM((2 * S, S), jnp.bfloat16),
                f32(S + DOWN2, wide),
                f32(DOWN2, wide),
                f32(RADIUS, wide),
                f32(S, 4 * LANES),
                f32(S, 4 * LANES),
                f32(S, LANES),
                dma((2 + per_dev,)),
                dma((2 + per_dev,)),
                dma((2 + per_dev,)),
                dma((2 + per_dev,)),
                dma((len(units), 4)),
                dma((len(units), 4)),
                dma((3,)),
                dma((3,)),
            ],
        ),
        out_shape=pltpu.VMEM((S, cols), jnp.float32),
        compiler_params=pltpu.CompilerParams(
            vmem_limit_bytes=56 * 1024 * 1024, collective_id=0, has_side_effects=True
        ),
        name="transport",
    )(*[x.swapaxes(1, 2) for x in (shifts_a, widths_a, shifts_b, widths_b)], source, boxes_a, boxes_a, boxes_b)


def solution(mesh):
    return jax.shard_map(
        functools.partial(on_device, mesh.shape["row"], mesh.shape["col"]),
        mesh=mesh,
        in_specs=(
            P("row", "col"),
            P("row", "col", None, None),
            P("row", "col", None),
            P("row", "col", None),
            P("row", "col", None, None),
            P("row", "col", None),
            P("row", "col", None),
        ),
        out_specs=P("row", "col"),
        check_vma=False,
    )
```

```python
import functools
import math

import jax
import jax.numpy as jnp
from jax import lax
from jax.experimental import pallas as pl
from jax.experimental.pallas import tpu as pltpu
from jax.sharding import PartitionSpec as P

S = 256
BOX = 512
ITERS = 3
RADIUS = 8
LANES = 128
HALF = S // 2
DOWN2 = HALF + RADIUS
TALL = RADIUS + 2 * S + DOWN2

kernel_eps = 0.05
blur_sigma = 2.0
blur_total = sum(
    math.exp(-(d * d) / (2.0 * blur_sigma * blur_sigma)) for d in range(-RADIUS, RADIUS + 1)
)


def gauss(offset):
    shape = (LANES, BOX + LANES)
    d = lax.broadcasted_iota(jnp.int32, shape, 1) - lax.broadcasted_iota(jnp.int32, shape, 0)
    g = gauss_of(offset - LANES + d)
    return jnp.concatenate([g[:, LANES:], g[:, :BOX]], axis=0)


def gauss_t(offset):
    shape = (BOX + LANES, LANES)
    d = lax.broadcasted_iota(jnp.int32, shape, 0) - lax.broadcasted_iota(jnp.int32, shape, 1)
    g = gauss_of(offset - LANES + d)
    return jnp.concatenate([g[LANES:], g[:BOX]], axis=1)


def gauss_of(d):
    dist = d.astype(jnp.float32) * (1.0 / S)
    return jnp.exp(dist * dist * (-1.0 / kernel_eps)).astype(jnp.bfloat16)


def blur_weight(d):
    f = d.astype(jnp.float32)
    w = jnp.exp(f * f * (-1.0 / (2.0 * blur_sigma * blur_sigma))) * (1.0 / blur_total)
    return jnp.where(jnp.abs(d) <= RADIUS, w, 0.0)


def split(x):
    hi = x.astype(jnp.bfloat16)
    return hi, (x - hi.astype(jnp.float32)).astype(jnp.bfloat16)


def dot(a, b):
    return jnp.dot(a, b, preferred_element_type=jnp.float32)


def dot_t(a, b):
    return lax.dot_general(a, b, (((1,), (1,)), ((), ())), preferred_element_type=jnp.float32)


def dot_split(a, b):
    (ah, al), (bh, bl) = a, b
    return dot(ah, bh) + (dot(ah, bl) + dot(al, bh))


def bf(x):
    return x.astype(jnp.bfloat16)


def target_of(box_ref, height, width):
    rows = lax.broadcasted_iota(jnp.int32, (BOX, BOX), 0)
    cols = lax.broadcasted_iota(jnp.int32, (BOX, BOX), 1)
    return jnp.where((rows < height) & (cols < width), box_ref[0, 0], 0.0)


MESH = pl.DeviceIdType.MESH
OWN = slice(RADIUS, RADIUS + S)


def tiles(first, count):
    return slice(first * LANES, (first + count) * LANES)


def plan_of(per_dev):
    last = per_dev - 1
    a_order = list(dict.fromkeys([0, last, min(1, last)] + list(range(per_dev - 2, 1, -1))))
    b_order = list(dict.fromkeys([last, last - 1, 0] + list(range(per_dev - 3, 0, -1))))
    steps = [("a", tuple(a_order[k : k + 2])) for k in range(0, per_dev, 2)]
    steps += [("b", (j,)) for j in b_order]
    n_tiles = 2 * per_dev + 3
    done, units, sent = [], [], set()
    for g, (kind, cells) in enumerate(steps):
        if kind == "a":
            continue
        done += cells
        ready = [
            t
            for t in range(n_tiles)
            if t not in sent
            and all(i in done for i in range(per_dev) if 2 * i <= t <= 2 * i + 4)
        ]
        sent.update(ready)
        runs = []
        for t in reversed(ready):
            if runs and runs[-1][0] == t + 1 and runs[-1][1] < 3:
                runs[-1] = (t, runs[-1][1] + 1)
            else:
                runs.append((t, 1))
        units += [(g, first, count) for first, count in runs]
    return steps, units


def kernel(
    per_dev,
    n_row,
    n_col,
    shifts_a,
    widths_a,
    shifts_b,
    widths_b,
    src,
    box_a,
    box_c,
    box_b,
    out,
    tgt,
    tgt_c,
    u_loc,
    mv_s,
    mv_u,
    canvas,
    band_hi,
    band_lo,
    r1,
    r2,
    rup,
    sb,
    cs,
    cl,
    s_send,
    s_recv,
    u_send,
    u_recv,
    x_send,
    x_recv,
    c_send,
    c_recv,
):
    g = pl.program_id(0)
    cols = per_dev * S
    n_tiles = 2 * per_dev + 3
    row, col = lax.axis_index("row"), lax.axis_index("col")
    odd = lax.rem(row, 2) == 1
    even = lax.rem(row, 2) == 0
    steps, units = plan_of(per_dev)
    n_steps = len(steps)

    def pick(values):
        res = jnp.int32(values[0])
        for k in range(1, n_steps):
            res = jnp.where(g == k, jnp.int32(values[k]), res)
        return res

    j, j_c = pick([c[0] for _, c in steps]), pick([c[-1] for _, c in steps])
    is_a = pick([int(k == "a") for k, _ in steps]) == 1

    def at(dr, dc):
        return (lax.rem(row + dr + n_row, n_row), lax.rem(col + dc + n_col, n_col))

    def remote(a, b, send, recv, to):
        return pltpu.make_async_remote_copy(
            src_ref=a, dst_ref=b, send_sem=send, recv_sem=recv, device_id=to, device_id_type=MESH
        )

    upper, lower = slice(0, HALF), slice(HALF, S)
    edge = slice(cols - LANES, cols)

    def halo(field, moved, k, send, recv):
        if k == 0:
            a, b, to = field.at[upper, :LANES], moved.at[lower, edge], at(-1, -1)
        elif k == 1:
            a, b, to = field.at[lower, :LANES], moved.at[upper, edge], at(0, -1)
        else:
            lo, hi = max((k - 2) * S, HALF), (k - 1) * S
            a, b, to = field.at[upper, lo:hi], moved.at[lower, lo - HALF : hi - HALF], at(-1, 0)
        return remote(a, b, send.at[k], recv.at[k], to)

    def mass(k):
        return halo(src, mv_s, k, s_send, s_recv)

    def scale(k):
        return halo(u_loc, mv_u, k, u_send, u_recv)

    near, far = RADIUS + S, RADIUS + 2 * S
    mid = near + DOWN2

    def spill(n, kind):
        _, first, count = units[n]
        c = tiles(first, count)
        a, b, to, k = {
            "even_far": (canvas.at[far:, c], r1.at[S:, c], at(1, 0), 0),
            "even_near": (canvas.at[near:far, c], r1.at[:S, c], at(1, 0), 1),
            "odd_near": (canvas.at[near:mid, c], r1.at[:DOWN2, c], at(1, 0), 0),
            "odd_mid": (canvas.at[mid:far, c], r1.at[DOWN2:S, c], at(1, 0), 1),
            "odd_far": (canvas.at[far:, c], r2.at[:, c], at(2, 0), 2),
            "up": (canvas.at[:RADIUS, c], rup.at[:, c], at(-1, 0), 3),
        }[kind]
        return remote(a, b, x_send.at[n, k], x_recv.at[n, k], to)

    flank = slice(0, 3 * LANES)
    tip = slice(3 * LANES, 4 * LANES)

    def beside(k):
        if k == 0:
            a, b, to = sb.at[:, flank], cs.at[:, flank], at(0, 1)
        elif k == 1:
            a, b, to = sb.at[:, tip], cs.at[:, tip], at(0, 1)
        else:
            a, b, to = sb.at[:, tip], cl, at(0, -1)
        return remote(a, b, c_send.at[k], c_recv.at[k], to)

    sides = 2 if n_col == 2 else 3

    def give(n):
        @pl.when(even)
        def _():
            spill(n, "even_far").start()
            spill(n, "even_near").start()

        @pl.when(odd)
        def _():
            spill(n, "odd_far").start()
            spill(n, "odd_mid").start()

        spill(n, "up").start()

    def hand_on(n):
        @pl.when(odd)
        def _():
            c = tiles(units[n][1], units[n][2])
            spill(n, "even_far").wait_recv()
            canvas[near:mid, c] += r1[S:, c]
            spill(n, "odd_near").start()

    def between():
        for k in range(1, n_steps):
            ready = [n for n, u in enumerate(units) if u[0] == k - 1]
            if ready:

                @pl.when(g == k)
                def _():
                    for n in ready:
                        hand_on(n)

    def fold(n):
        c = tiles(units[n][1], units[n][2])

        @pl.when(even)
        def _():
            spill(n, "odd_near").wait_recv()
            spill(n, "odd_mid").wait_recv()
            canvas[OWN, c] += r1[:S, c]

        @pl.when(odd)
        def _():
            spill(n, "even_near").wait_recv()
            spill(n, "odd_far").wait_recv()
            canvas[OWN, c] += r1[:S, c]
            canvas[RADIUS : RADIUS + DOWN2, c] += r2[:, c]

        spill(n, "up").wait_recv()
        canvas[S : RADIUS + S, c] += rup[:, c]

    def smooth(first, count):
        lo, hi = max(first - 1, 0), min(first + count + 1, n_tiles)
        rows = slice((lo - first + 1) * LANES, (hi - first + 1) * LANES)
        field = split(canvas[OWN, lo * LANES : hi * LANES])
        return dot_split(field, [b[rows, : count * LANES] for b in (band_hi, band_lo)])

    def the_band():
        n = lax.broadcasted_iota(jnp.int32, (2 * S, S), 0)
        m = lax.broadcasted_iota(jnp.int32, (2 * S, S), 1)
        return split(blur_weight(n - LANES - m))

    @pl.when(is_a)
    def _():
        barrier = pltpu.get_barrier_semaphore()
        peers = [(-1, 0), (1, 0), (-2, 0), (2, 0), (0, -1), (0, 1), (-1, -1), (1, 1)]

        @pl.when(g == 0)
        def _():
            for dr, dc in peers:
                pl.semaphore_signal(barrier, inc=1, device_id=at(dr, dc), device_id_type=MESH)
            mv_s[upper, : cols - HALF] = src[lower, HALF:]
            canvas[...] = jnp.zeros_like(canvas)
            band_hi[...], band_lo[...] = the_band()

        cells = []
        for c, box, t in ((j, box_a, tgt), (j_c, box_c, tgt_c)):
            o_r, o_c = shifts_a[0, 0, c], shifts_a[0, 1, c]
            h, w = widths_a[0, 0, c], widths_a[0, 1, c]
            krt, kc = gauss_t(o_r), gauss(o_c)
            t[...] = target_of(box, h, w)
            here = pl.ds(pl.multiple_of(c * S, S), S)
            in_r = bf(jnp.sum(krt.astype(jnp.float32), axis=1, keepdims=True)).astype(jnp.float32)
            in_c = jnp.sum(kc.astype(jnp.float32), axis=0, keepdims=True)
            cells.append((gauss(o_r), krt, kc, t, src[:, here], here, in_r * in_c))
        back = [c[-1] for c in cells]
        for step in range(ITERS):
            v = [bf(c[3][...] / b) for c, b in zip(cells, back)]
            inner = [bf(dot(c[0], x)) for c, x in zip(cells, v)]
            u = [c[4] / dot_t(x, c[2]) for c, x in zip(cells, inner)]
            if step < ITERS - 1:
                inner = [bf(dot(c[1], bf(x))) for c, x in zip(cells, u)]
                back = [dot(x, c[2]) for c, x in zip(cells, inner)]
            if step == 0:

                @pl.when(g == 0)
                def _():
                    pl.semaphore_wait(barrier, len(peers))
                    for k in (0, 1, 1 + per_dev, 2):
                        mass(k).start()

        for c, x in zip(cells, u):
            u_loc[:, c[5]] = x

        for n, (kind, pair) in enumerate(steps):
            if kind == "b":
                continue

            @pl.when(g == n)
            def _():
                if n == 0:
                    scale(0).start()
                    scale(1).start()
                for i in reversed(pair):
                    scale(2 + i).start()
                if n == 0:
                    for k in range(per_dev, 2, -1):
                        mass(k).start()
                for i in pair:
                    lo, hi = max(i * S, HALF), (i + 1) * S
                    mv_u[upper, lo - HALF : hi - HALF] = u_loc[lower, lo:hi]

    @pl.when(jnp.logical_not(is_a))
    def _():
        waited = set()
        for k, (kind, pair) in enumerate(steps):
            if kind == "a":
                continue
            (i,) = pair
            need = [2 + c for c in (i, i + 1) if c < per_dev]
            need = [c for c in need + [0, 1] * (i == per_dev - 1) if c not in waited]
            waited.update(need)

            @pl.when(g == k)
            def _():
                for c in need:
                    mass(c).wait_recv()
                    scale(c).wait_recv()

        o_r, o_c = shifts_b[0, 0, j], shifts_b[0, 1, j]
        h, w = widths_b[0, 0, j], widths_b[0, 1, j]
        kr = gauss(o_r)
        krt = gauss_t(o_r)
        kc = gauss(o_c)
        tgt[...] = target_of(box_b, h, w)
        here = pl.ds(pl.multiple_of(j * S, S), S)
        a = mv_s[:, here]
        u = mv_u[:, here]
        for step in range(ITERS):
            back = dot(bf(dot(krt, bf(u))), kc)
            v = tgt[...] / back
            u = a / dot_t(bf(dot(kr, bf(v))), kc)
            if step == 0:
                between()

        plan = v * dot(bf(dot(krt, bf(u))), kc)

        r = lax.broadcasted_iota(jnp.int32, (LANES, 3 * LANES), 0) - RADIUS
        m = lax.broadcasted_iota(jnp.int32, (LANES, 3 * LANES), 1) - 2 * LANES
        weights = split(blur_weight(HALF + o_r + m - r))
        halves = split(plan)
        parts = []
        for b in range(-(-TALL // LANES)):
            height = min(LANES, TALL - b * LANES)
            lo, hi = max(b - 2, 0), min(b + 1, BOX // LANES)
            wt = slice((lo - b + 2) * LANES, (hi - b + 2) * LANES)
            parts.append(
                dot_split(
                    [x[:height, wt] for x in weights],
                    [x[lo * LANES : hi * LANES] for x in halves],
                )
            )
        rowed = jnp.concatenate(parts, axis=0)
        s = HALF + o_c
        lane = lax.broadcasted_iota(jnp.int32, (TALL, LANES), 1)
        turned = [pltpu.roll(rowed[:, tiles(t, 1)], s, 1) for t in range(BOX // LANES)]
        zero = jnp.zeros((TALL, LANES), jnp.float32)
        for t in range(BOX // LANES + 1):
            left = turned[t - 1] if t > 0 else zero
            right = turned[t] if t < BOX // LANES else zero
            spot = pl.ds(pl.multiple_of(j * S + t * LANES, LANES), LANES)
            canvas[:, spot] += jnp.where(lane < s, left, right)

        for k in range(n_steps):
            ready = [n for n, u_ in enumerate(units) if u_[0] == k]
            if ready:

                @pl.when(g == k)
                def _():
                    for n in ready:
                        give(n)

        @pl.when(g == n_steps - 1)
        def _():
            final = [n for n, u_ in enumerate(units) if u_[0] == n_steps - 1]
            early = [n for n in range(len(units)) if n not in final]
            first = 2 * per_dev
            ready = set()

            def settle(need):
                while not need <= ready:
                    n = early.pop(0)
                    fold(n)
                    ready.update(range(units[n][1], units[n][1] + units[n][2]))

            settle({n_tiles - 1})
            for n in final:
                hand_on(n)
            settle(set(range(first - 1, n_tiles)))
            sb[:, 2 * LANES : 3 * LANES] = smooth(first + 2, 1)
            sb[:, : 2 * LANES] = smooth(first, 2)
            beside(0).start()
            settle({0})
            over = split(canvas[OWN, tiles(n_tiles - 1, 1)])
            under = split(canvas[OWN, tiles(0, 1)])
            sb[:, tip] = dot_split(over, [b[:LANES, :LANES] for b in (band_hi, band_lo)]) + dot_split(
                under, [b[2 * LANES : 3 * LANES, :LANES] for b in (band_hi, band_lo)]
            )
            for k in range(1, sides):
                beside(k).start()
            while early:
                settle({units[early[0]][1]})
            shown = set()

            def show():
                t = 2 * per_dev - 1
                while t >= 0:
                    ok = lambda x: x not in shown and all(
                        y in ready for y in (x - 1, x, x + 1) if 0 <= y < n_tiles
                    )
                    if ok(t):
                        count = 2 if t > 0 and ok(t - 1) else 1
                        base = t - count + 1
                        out[:, tiles(base, count)] = smooth(base, count)
                        shown.update(range(base, t + 1))
                        t -= count
                    else:
                        t -= 1

            show()
            for n in final:
                fold(n)
                ready.update(range(units[n][1], units[n][1] + units[n][2]))
                show()

            ln = lax.broadcasted_iota(jnp.int32, (S, LANES), 1)
            for k in range(sides):
                beside(k).wait_recv()
            out[:, flank] += cs[:, flank]
            out[:, tip] += jnp.where(ln < LANES - RADIUS, cs[:, tip], 0.0)
            behind = cs[:, tip] if n_col == 2 else cl[...]
            out[:, edge] += jnp.where(ln >= LANES - RADIUS, behind, 0.0)

            for k in range(2 + per_dev):
                mass(k).wait_send()
                scale(k).wait_send()
            for k in range(sides):
                beside(k).wait_send()
            for n in range(len(units)):
                spill(n, "up").wait_send()

                @pl.when(even)
                def _():
                    spill(n, "even_far").wait_send()
                    spill(n, "even_near").wait_send()

                @pl.when(odd)
                def _():
                    spill(n, "odd_near").wait_send()
                    spill(n, "odd_mid").wait_send()
                    spill(n, "odd_far").wait_send()


def on_device(n_row, n_col, source, boxes_a, shifts_a, widths_a, boxes_b, shifts_b, widths_b):
    cols = source.shape[1]
    per_dev = cols // S
    wide = cols + 3 * LANES
    steps, units = plan_of(per_dev)
    f32 = lambda *shape: pltpu.VMEM(shape, jnp.float32)
    dma = pltpu.SemaphoreType.DMA
    box = (1, 1, BOX, BOX)

    def boxes_of(kind, side):
        def where(g):
            block = None
            for k in range(len(steps) - 1, -1, -1):
                if steps[k][0] != kind:
                    continue
                cell = steps[k][1][side]
                block = jnp.int32(cell) if block is None else jnp.where(g <= k, cell, block)
            return (0, block, 0, 0)

        return pl.BlockSpec(box, where)

    smem = pl.BlockSpec(memory_space=pltpu.SMEM)
    return pl.pallas_call(
        functools.partial(kernel, per_dev, n_row, n_col),
        grid_spec=pltpu.PrefetchScalarGridSpec(
            num_scalar_prefetch=0,
            grid=(len(steps),),
            in_specs=[
                smem,
                smem,
                smem,
                smem,
                pl.BlockSpec((S, cols), lambda g: (0, 0)),
                boxes_of("a", 0),
                boxes_of("a", -1),
                boxes_of("b", 0),
            ],
            out_specs=pl.BlockSpec(memory_space=pltpu.VMEM),
            scratch_shapes=[
                f32(BOX, BOX),
                f32(BOX, BOX),
                f32(S, cols),
                f32(S, cols),
                f32(S, cols),
                f32(TALL, wide),
                pltpu.VMEM((2 * S, S), jnp.bfloat16),
                pltpu.VMEM((2 * S, S), jnp.bfloat16),
                f32(S + DOWN2, wide),
                f32(DOWN2, wide),
                f32(RADIUS, wide),
                f32(S, 4 * LANES),
                f32(S, 4 * LANES),
                f32(S, LANES),
                dma((2 + per_dev,)),
                dma((2 + per_dev,)),
                dma((2 + per_dev,)),
                dma((2 + per_dev,)),
                dma((len(units), 4)),
                dma((len(units), 4)),
                dma((3,)),
                dma((3,)),
            ],
        ),
        out_shape=pltpu.VMEM((S, cols), jnp.float32),
        compiler_params=pltpu.CompilerParams(
            vmem_limit_bytes=56 * 1024 * 1024, collective_id=0, has_side_effects=True
        ),
        name="transport",
    )(*[x.swapaxes(1, 2) for x in (shifts_a, widths_a, shifts_b, widths_b)], source, boxes_a, boxes_a, boxes_b)


def solution(mesh):
    return jax.shard_map(
        functools.partial(on_device, mesh.shape["row"], mesh.shape["col"]),
        mesh=mesh,
        in_specs=(
            P("row", "col"),
            P("row", "col", None, None),
            P("row", "col", None),
            P("row", "col", None),
            P("row", "col", None, None),
            P("row", "col", None),
            P("row", "col", None),
        ),
        out_specs=P("row", "col"),
        check_vma=False,
    )
```

```python
import functools
import math

import jax
import jax.numpy as jnp
from jax import lax
from jax.experimental import pallas as pl
from jax.experimental.pallas import tpu as pltpu
from jax.sharding import PartitionSpec as P

S = 256
BOX = 512
ITERS = 3
RADIUS = 8
LANES = 128
HALF = S // 2
DOWN2 = HALF + RADIUS
TALL = RADIUS + 2 * S + DOWN2

kernel_eps = 0.05
blur_sigma = 2.0
blur_total = sum(
    math.exp(-(d * d) / (2.0 * blur_sigma * blur_sigma)) for d in range(-RADIUS, RADIUS + 1)
)


def gauss(offset):
    shape = (LANES, BOX + LANES)
    d = lax.broadcasted_iota(jnp.int32, shape, 1) - lax.broadcasted_iota(jnp.int32, shape, 0)
    g = gauss_of(offset - LANES + d)
    return jnp.concatenate([g[:, LANES:], g[:, :BOX]], axis=0)


def gauss_t(offset):
    shape = (BOX + LANES, LANES)
    d = lax.broadcasted_iota(jnp.int32, shape, 0) - lax.broadcasted_iota(jnp.int32, shape, 1)
    g = gauss_of(offset - LANES + d)
    return jnp.concatenate([g[LANES:], g[:BOX]], axis=1)


def gauss_of(d):
    dist = d.astype(jnp.float32) * (1.0 / S)
    return jnp.exp(dist * dist * (-1.0 / kernel_eps)).astype(jnp.bfloat16)


def blur_weight(d):
    f = d.astype(jnp.float32)
    w = jnp.exp(f * f * (-1.0 / (2.0 * blur_sigma * blur_sigma))) * (1.0 / blur_total)
    return jnp.where(jnp.abs(d) <= RADIUS, w, 0.0)


def split(x):
    hi = x.astype(jnp.bfloat16)
    return hi, (x - hi.astype(jnp.float32)).astype(jnp.bfloat16)


def dot(a, b):
    return jnp.dot(a, b, preferred_element_type=jnp.float32)


def dot_t(a, b):
    return lax.dot_general(a, b, (((1,), (1,)), ((), ())), preferred_element_type=jnp.float32)


def dot_split(a, b):
    (ah, al), (bh, bl) = a, b
    return dot(ah, bh) + (dot(ah, bl) + dot(al, bh))


def bf(x):
    return x.astype(jnp.bfloat16)


def target_of(box, height, width):
    rows = lax.broadcasted_iota(jnp.int32, (BOX, BOX), 0)
    cols = lax.broadcasted_iota(jnp.int32, (BOX, BOX), 1)
    return jnp.where((rows < height) & (cols < width), box, 0.0)


MESH = pl.DeviceIdType.MESH
OWN = slice(RADIUS, RADIUS + S)


def tiles(first, count):
    return slice(first * LANES, (first + count) * LANES)


def plan_of(per_dev):
    last = per_dev - 1
    a_order = list(dict.fromkeys([0, last, min(1, last)] + list(range(per_dev - 2, 1, -1))))
    b_order = list(dict.fromkeys([last, last - 1, 0] + list(range(per_dev - 3, 0, -1))))
    steps = [("a", tuple(a_order[k : k + 2])) for k in range(0, per_dev, 2)]
    steps += [("b", (j,)) for j in b_order]
    n_tiles = 2 * per_dev + 3
    done, units, sent = [], [], set()
    for g, (kind, cells) in enumerate(steps):
        if kind == "a":
            continue
        done += cells
        ready = [
            t
            for t in range(n_tiles)
            if t not in sent
            and all(i in done for i in range(per_dev) if 2 * i <= t <= 2 * i + 4)
        ]
        sent.update(ready)
        runs = []
        for t in reversed(ready):
            if runs and runs[-1][0] == t + 1 and runs[-1][1] < 3:
                runs[-1] = (t, runs[-1][1] + 1)
            else:
                runs.append((t, 1))
        units += [(g, first, count) for first, count in runs]
    return steps, units


def kernel(
    per_dev,
    n_row,
    n_col,
    shifts_a,
    widths_a,
    shifts_b,
    widths_b,
    src_hbm,
    hbm_a,
    hbm_b,
    out,
    src,
    boxes,
    tgt,
    tgt_c,
    u_loc,
    mv_s,
    mv_u,
    canvas,
    band_hi,
    band_lo,
    r1,
    r2,
    rup,
    sb,
    cs,
    cl,
    s_send,
    s_recv,
    u_send,
    u_recv,
    x_send,
    x_recv,
    c_send,
    c_recv,
    b_sem,
):
    g = pl.program_id(0)
    cols = per_dev * S
    n_tiles = 2 * per_dev + 3
    row, col = lax.axis_index("row"), lax.axis_index("col")
    odd = lax.rem(row, 2) == 1
    even = lax.rem(row, 2) == 0
    steps, units = plan_of(per_dev)
    n_steps = len(steps)

    def pick(values):
        res = jnp.int32(values[0])
        for k in range(1, n_steps):
            res = jnp.where(g == k, jnp.int32(values[k]), res)
        return res

    j, j_c = pick([c[0] for _, c in steps]), pick([c[-1] for _, c in steps])
    is_a = pick([int(k == "a") for k, _ in steps]) == 1
    slots, held = [], []
    for kind, pair in steps:
        slots.append(range(len(held), len(held) + len(pair)))
        held += [(kind, i) for i in pair]
    slot, slot_c = pick([k[0] for k in slots]), pick([k[-1] for k in slots])

    def fetch(k):
        if k == len(held):
            return pltpu.make_async_copy(src_hbm, src, b_sem.at[k])
        kind, i = held[k]
        hbm = hbm_a if kind == "a" else hbm_b
        return pltpu.make_async_copy(hbm.at[0, i], boxes.at[k], b_sem.at[k])

    def at(dr, dc):
        return (lax.rem(row + dr + n_row, n_row), lax.rem(col + dc + n_col, n_col))

    def remote(a, b, send, recv, to):
        return pltpu.make_async_remote_copy(
            src_ref=a, dst_ref=b, send_sem=send, recv_sem=recv, device_id=to, device_id_type=MESH
        )

    upper, lower = slice(0, HALF), slice(HALF, S)
    edge = slice(cols - LANES, cols)

    def halo(field, moved, k, send, recv):
        if k == 0:
            a, b, to = field.at[upper, :LANES], moved.at[lower, edge], at(-1, -1)
        elif k == 1:
            a, b, to = field.at[lower, :LANES], moved.at[upper, edge], at(0, -1)
        else:
            lo, hi = max((k - 2) * S, HALF), (k - 1) * S
            a, b, to = field.at[upper, lo:hi], moved.at[lower, lo - HALF : hi - HALF], at(-1, 0)
        return remote(a, b, send.at[k], recv.at[k], to)

    def mass(k):
        return halo(src, mv_s, k, s_send, s_recv)

    def scale(k):
        return halo(u_loc, mv_u, k, u_send, u_recv)

    near, far = RADIUS + S, RADIUS + 2 * S
    mid = near + DOWN2

    def spill(n, kind):
        _, first, count = units[n]
        c = tiles(first, count)
        a, b, to, k = {
            "even_far": (canvas.at[far:, c], r1.at[S:, c], at(1, 0), 0),
            "even_near": (canvas.at[near:far, c], r1.at[:S, c], at(1, 0), 1),
            "odd_near": (canvas.at[near:mid, c], r1.at[:DOWN2, c], at(1, 0), 0),
            "odd_mid": (canvas.at[mid:far, c], r1.at[DOWN2:S, c], at(1, 0), 1),
            "odd_far": (canvas.at[far:, c], r2.at[:, c], at(2, 0), 2),
            "up": (canvas.at[:RADIUS, c], rup.at[:, c], at(-1, 0), 3),
        }[kind]
        return remote(a, b, x_send.at[n, k], x_recv.at[n, k], to)

    flank = slice(0, 3 * LANES)
    tip = slice(3 * LANES, 4 * LANES)

    def beside(k):
        if k == 0:
            a, b, to = sb.at[:, flank], cs.at[:, flank], at(0, 1)
        elif k == 1:
            a, b, to = sb.at[:, tip], cs.at[:, tip], at(0, 1)
        else:
            a, b, to = sb.at[:, tip], cl, at(0, -1)
        return remote(a, b, c_send.at[k], c_recv.at[k], to)

    sides = 2 if n_col == 2 else 3

    def give(n):
        @pl.when(even)
        def _():
            spill(n, "even_far").start()
            spill(n, "even_near").start()

        @pl.when(odd)
        def _():
            spill(n, "odd_far").start()
            spill(n, "odd_mid").start()

        spill(n, "up").start()

    def hand_on(n):
        @pl.when(odd)
        def _():
            c = tiles(units[n][1], units[n][2])
            spill(n, "even_far").wait_recv()
            canvas[near:mid, c] += r1[S:, c]
            spill(n, "odd_near").start()

    def between():
        for k in range(1, n_steps):
            ready = [n for n, u in enumerate(units) if u[0] == k - 1]
            if ready:

                @pl.when(g == k)
                def _():
                    for n in ready:
                        hand_on(n)

    def fold(n):
        c = tiles(units[n][1], units[n][2])

        @pl.when(even)
        def _():
            spill(n, "odd_near").wait_recv()
            spill(n, "odd_mid").wait_recv()
            canvas[OWN, c] += r1[:S, c]

        @pl.when(odd)
        def _():
            spill(n, "even_near").wait_recv()
            spill(n, "odd_far").wait_recv()
            canvas[OWN, c] += r1[:S, c]
            canvas[RADIUS : RADIUS + DOWN2, c] += r2[:, c]

        spill(n, "up").wait_recv()
        canvas[S : RADIUS + S, c] += rup[:, c]

    def smooth(first, count):
        lo, hi = max(first - 1, 0), min(first + count + 1, n_tiles)
        rows = slice((lo - first + 1) * LANES, (hi - first + 1) * LANES)
        field = split(canvas[OWN, lo * LANES : hi * LANES])
        return dot_split(field, [b[rows, : count * LANES] for b in (band_hi, band_lo)])

    def the_band():
        n = lax.broadcasted_iota(jnp.int32, (2 * S, S), 0)
        m = lax.broadcasted_iota(jnp.int32, (2 * S, S), 1)
        return split(blur_weight(n - LANES - m))

    @pl.when(is_a)
    def _():
        barrier = pltpu.get_barrier_semaphore()
        peers = [(-1, 0), (1, 0), (-2, 0), (2, 0), (0, -1), (0, 1), (-1, -1), (1, 1)]

        @pl.when(g == 0)
        def _():
            for dr, dc in peers:
                pl.semaphore_signal(barrier, inc=1, device_id=at(dr, dc), device_id_type=MESH)
            for k in slots[0]:
                fetch(k).start()
            fetch(len(held)).start()
            for k in range(slots[1][0], len(held)):
                fetch(k).start()
            canvas[...] = jnp.zeros_like(canvas)
            band_hi[...], band_lo[...] = the_band()

        cells = []
        for c in (j, j_c):
            o_r, o_c = shifts_a[0, 0, c], shifts_a[0, 1, c]
            krt, kc = gauss_t(o_r), gauss(o_c)
            in_r = bf(jnp.sum(krt.astype(jnp.float32), axis=1, keepdims=True)).astype(jnp.float32)
            in_c = jnp.sum(kc.astype(jnp.float32), axis=0, keepdims=True)
            cells.append((gauss(o_r), krt, kc, in_r * in_c))

        for n, (kind, _) in enumerate(steps):
            if kind == "a":

                @pl.when(g == n)
                def _():
                    for k in slots[n]:
                        fetch(k).wait()
                    if n == 0:
                        fetch(len(held)).wait()
                        mv_s[upper, : cols - HALF] = src[lower, HALF:]

        for n, (c, k, t) in enumerate(((j, slot, tgt), (j_c, slot_c, tgt_c))):
            t[...] = target_of(boxes[k], widths_a[0, 0, c], widths_a[0, 1, c])
            here = pl.ds(pl.multiple_of(c * S, S), S)
            kr, krt, kc, first = cells[n]
            cells[n] = (kr, krt, kc, t, src[:, here], here, first)
        back = [c[-1] for c in cells]
        for step in range(ITERS):
            v = [bf(c[3][...] / b) for c, b in zip(cells, back)]
            inner = [bf(dot(c[0], x)) for c, x in zip(cells, v)]
            u = [c[4] / dot_t(x, c[2]) for c, x in zip(cells, inner)]
            if step < ITERS - 1:
                inner = [bf(dot(c[1], bf(x))) for c, x in zip(cells, u)]
                back = [dot(x, c[2]) for c, x in zip(cells, inner)]
            if step == 0:

                @pl.when(g == 0)
                def _():
                    pl.semaphore_wait(barrier, len(peers))
                    for k in (0, 1, 1 + per_dev, 2):
                        mass(k).start()

        for c, x in zip(cells, u):
            u_loc[:, c[5]] = x

        for n, (kind, pair) in enumerate(steps):
            if kind == "b":
                continue

            @pl.when(g == n)
            def _():
                if n == 0:
                    scale(0).start()
                    scale(1).start()
                for i in reversed(pair):
                    scale(2 + i).start()
                if n == 0:
                    for k in range(per_dev, 2, -1):
                        mass(k).start()
                for i in pair:
                    lo, hi = max(i * S, HALF), (i + 1) * S
                    mv_u[upper, lo - HALF : hi - HALF] = u_loc[lower, lo:hi]

    @pl.when(jnp.logical_not(is_a))
    def _():
        waited = set()
        for k, (kind, pair) in enumerate(steps):
            if kind == "a":
                continue
            (i,) = pair
            need = [2 + c for c in (i, i + 1) if c < per_dev]
            need = [c for c in need + [0, 1] * (i == per_dev - 1) if c not in waited]
            waited.update(need)

            @pl.when(g == k)
            def _():
                fetch(slots[k][0]).wait()
                for c in need:
                    mass(c).wait_recv()
                    scale(c).wait_recv()

        o_r, o_c = shifts_b[0, 0, j], shifts_b[0, 1, j]
        h, w = widths_b[0, 0, j], widths_b[0, 1, j]
        kr = gauss(o_r)
        krt = gauss_t(o_r)
        kc = gauss(o_c)
        tgt[...] = target_of(boxes[slot], h, w)
        here = pl.ds(pl.multiple_of(j * S, S), S)
        a = mv_s[:, here]
        u = mv_u[:, here]
        for step in range(ITERS):
            back = dot(bf(dot(krt, bf(u))), kc)
            v = tgt[...] / back
            u = a / dot_t(bf(dot(kr, bf(v))), kc)
            if step == 0:
                between()

        plan = v * dot(bf(dot(krt, bf(u))), kc)

        r = lax.broadcasted_iota(jnp.int32, (LANES, 3 * LANES), 0) - RADIUS
        m = lax.broadcasted_iota(jnp.int32, (LANES, 3 * LANES), 1) - 2 * LANES
        weights = split(blur_weight(HALF + o_r + m - r))
        halves = split(plan)
        parts = []
        for b in range(-(-TALL // LANES)):
            height = min(LANES, TALL - b * LANES)
            lo, hi = max(b - 2, 0), min(b + 1, BOX // LANES)
            wt = slice((lo - b + 2) * LANES, (hi - b + 2) * LANES)
            parts.append(
                dot_split(
                    [x[:height, wt] for x in weights],
                    [x[lo * LANES : hi * LANES] for x in halves],
                )
            )
        rowed = jnp.concatenate(parts, axis=0)
        s = HALF + o_c
        lane = lax.broadcasted_iota(jnp.int32, (TALL, LANES), 1)
        turned = [pltpu.roll(rowed[:, tiles(t, 1)], s, 1) for t in range(BOX // LANES)]
        zero = jnp.zeros((TALL, LANES), jnp.float32)
        for t in range(BOX // LANES + 1):
            left = turned[t - 1] if t > 0 else zero
            right = turned[t] if t < BOX // LANES else zero
            spot = pl.ds(pl.multiple_of(j * S + t * LANES, LANES), LANES)
            canvas[:, spot] += jnp.where(lane < s, left, right)

        for k in range(n_steps):
            ready = [n for n, u_ in enumerate(units) if u_[0] == k]
            if ready:

                @pl.when(g == k)
                def _():
                    for n in ready:
                        give(n)

        @pl.when(g == n_steps - 1)
        def _():
            final = [n for n, u_ in enumerate(units) if u_[0] == n_steps - 1]
            early = [n for n in range(len(units)) if n not in final]
            first = 2 * per_dev
            ready = set()

            def settle(need):
                while not need <= ready:
                    n = early.pop(0)
                    fold(n)
                    ready.update(range(units[n][1], units[n][1] + units[n][2]))

            settle({n_tiles - 1})
            for n in final:
                hand_on(n)
            settle(set(range(first - 1, n_tiles)))
            sb[:, 2 * LANES : 3 * LANES] = smooth(first + 2, 1)
            sb[:, : 2 * LANES] = smooth(first, 2)
            beside(0).start()
            settle({0})
            over = split(canvas[OWN, tiles(n_tiles - 1, 1)])
            under = split(canvas[OWN, tiles(0, 1)])
            sb[:, tip] = dot_split(over, [b[:LANES, :LANES] for b in (band_hi, band_lo)]) + dot_split(
                under, [b[2 * LANES : 3 * LANES, :LANES] for b in (band_hi, band_lo)]
            )
            for k in range(1, sides):
                beside(k).start()
            while early:
                settle({units[early[0]][1]})
            shown = set()

            def show():
                t = 2 * per_dev - 1
                while t >= 0:
                    ok = lambda x: x not in shown and all(
                        y in ready for y in (x - 1, x, x + 1) if 0 <= y < n_tiles
                    )
                    if ok(t):
                        count = 2 if t > 0 and ok(t - 1) else 1
                        base = t - count + 1
                        out[:, tiles(base, count)] = smooth(base, count)
                        shown.update(range(base, t + 1))
                        t -= count
                    else:
                        t -= 1

            show()
            for n in final:
                fold(n)
                ready.update(range(units[n][1], units[n][1] + units[n][2]))
                show()

            ln = lax.broadcasted_iota(jnp.int32, (S, LANES), 1)
            for k in range(sides):
                beside(k).wait_recv()
            out[:, flank] += cs[:, flank]
            out[:, tip] += jnp.where(ln < LANES - RADIUS, cs[:, tip], 0.0)
            behind = cs[:, tip] if n_col == 2 else cl[...]
            out[:, edge] += jnp.where(ln >= LANES - RADIUS, behind, 0.0)

            for k in range(2 + per_dev):
                mass(k).wait_send()
                scale(k).wait_send()
            for k in range(sides):
                beside(k).wait_send()
            for n in range(len(units)):
                spill(n, "up").wait_send()

                @pl.when(even)
                def _():
                    spill(n, "even_far").wait_send()
                    spill(n, "even_near").wait_send()

                @pl.when(odd)
                def _():
                    spill(n, "odd_near").wait_send()
                    spill(n, "odd_mid").wait_send()
                    spill(n, "odd_far").wait_send()


def on_device(n_row, n_col, source, boxes_a, shifts_a, widths_a, boxes_b, shifts_b, widths_b):
    cols = source.shape[1]
    per_dev = cols // S
    wide = cols + 3 * LANES
    steps, units = plan_of(per_dev)
    f32 = lambda *shape: pltpu.VMEM(shape, jnp.float32)
    dma = pltpu.SemaphoreType.DMA
    smem = pl.BlockSpec(memory_space=pltpu.SMEM)
    return pl.pallas_call(
        functools.partial(kernel, per_dev, n_row, n_col),
        grid_spec=pltpu.PrefetchScalarGridSpec(
            num_scalar_prefetch=0,
            grid=(len(steps),),
            in_specs=[
                smem,
                smem,
                smem,
                smem,
                *[pl.BlockSpec(memory_space=pl.ANY)] * 3,
            ],
            out_specs=pl.BlockSpec(memory_space=pltpu.VMEM),
            scratch_shapes=[
                f32(S, cols),
                f32(2 * per_dev, BOX, BOX),
                f32(BOX, BOX),
                f32(BOX, BOX),
                f32(S, cols),
                f32(S, cols),
                f32(S, cols),
                f32(TALL, wide),
                pltpu.VMEM((2 * S, S), jnp.bfloat16),
                pltpu.VMEM((2 * S, S), jnp.bfloat16),
                f32(S + DOWN2, wide),
                f32(DOWN2, wide),
                f32(RADIUS, wide),
                f32(S, 4 * LANES),
                f32(S, 4 * LANES),
                f32(S, LANES),
                dma((2 + per_dev,)),
                dma((2 + per_dev,)),
                dma((2 + per_dev,)),
                dma((2 + per_dev,)),
                dma((len(units), 4)),
                dma((len(units), 4)),
                dma((3,)),
                dma((3,)),
                dma((2 * per_dev + 1,)),
            ],
        ),
        out_shape=pltpu.VMEM((S, cols), jnp.float32),
        compiler_params=pltpu.CompilerParams(
            vmem_limit_bytes=56 * 1024 * 1024, collective_id=0, has_side_effects=True
        ),
        name="transport",
    )(*[x.swapaxes(1, 2) for x in (shifts_a, widths_a, shifts_b, widths_b)], source, boxes_a, boxes_b)


def solution(mesh):
    return jax.shard_map(
        functools.partial(on_device, mesh.shape["row"], mesh.shape["col"]),
        mesh=mesh,
        in_specs=(
            P("row", "col"),
            P("row", "col", None, None),
            P("row", "col", None),
            P("row", "col", None),
            P("row", "col", None, None),
            P("row", "col", None),
            P("row", "col", None),
        ),
        out_specs=P("row", "col"),
        check_vma=False,
    )
```

```python
import functools
import math

import jax
import jax.numpy as jnp
from jax import lax
from jax.experimental import pallas as pl
from jax.experimental.pallas import tpu as pltpu
from jax.sharding import PartitionSpec as P

S = 256
BOX = 512
ITERS = 3
RADIUS = 8
LANES = 128
HALF = S // 2
DOWN2 = HALF + RADIUS
TALL = RADIUS + 2 * S + DOWN2

kernel_eps = 0.05
blur_sigma = 2.0
blur_total = sum(
    math.exp(-(d * d) / (2.0 * blur_sigma * blur_sigma)) for d in range(-RADIUS, RADIUS + 1)
)


def gauss(offset):
    shape = (LANES, BOX + LANES)
    d = lax.broadcasted_iota(jnp.int32, shape, 1) - lax.broadcasted_iota(jnp.int32, shape, 0)
    g = gauss_of(offset - LANES + d)
    return jnp.concatenate([g[:, LANES:], g[:, :BOX]], axis=0)


def gauss_t(offset):
    shape = (BOX + LANES, LANES)
    d = lax.broadcasted_iota(jnp.int32, shape, 0) - lax.broadcasted_iota(jnp.int32, shape, 1)
    g = gauss_of(offset - LANES + d)
    return jnp.concatenate([g[LANES:], g[:BOX]], axis=1)


def gauss_of(d):
    dist = d.astype(jnp.float32) * (1.0 / S)
    return jnp.exp(dist * dist * (-1.0 / kernel_eps)).astype(jnp.bfloat16)


def blur_weight(d):
    f = d.astype(jnp.float32)
    w = jnp.exp(f * f * (-1.0 / (2.0 * blur_sigma * blur_sigma))) * (1.0 / blur_total)
    return jnp.where(jnp.abs(d) <= RADIUS, w, 0.0)


def split(x):
    hi = x.astype(jnp.bfloat16)
    return hi, (x - hi.astype(jnp.float32)).astype(jnp.bfloat16)


def dot(a, b):
    return jnp.dot(a, b, preferred_element_type=jnp.float32)


def dot_t(a, b):
    return lax.dot_general(a, b, (((1,), (1,)), ((), ())), preferred_element_type=jnp.float32)


def dot_split(a, b):
    (ah, al), (bh, bl) = a, b
    both = dot(jnp.concatenate([ah, al], axis=0), bh)
    return both[: ah.shape[0]] + (both[ah.shape[0] :] + dot(ah, bl))


def bf(x):
    return x.astype(jnp.bfloat16)


def target_of(box, height, width):
    rows = lax.broadcasted_iota(jnp.int32, (BOX, BOX), 0)
    cols = lax.broadcasted_iota(jnp.int32, (BOX, BOX), 1)
    return jnp.where((rows < height) & (cols < width), box, 0.0)


MESH = pl.DeviceIdType.MESH
OWN = slice(RADIUS, RADIUS + S)


def tiles(first, count):
    return slice(first * LANES, (first + count) * LANES)


def plan_of(per_dev):
    last = per_dev - 1
    a_order = list(dict.fromkeys([0, last, min(1, last)] + list(range(per_dev - 2, 1, -1))))
    b_order = list(dict.fromkeys([last, last - 1, 0] + list(range(per_dev - 3, 0, -1))))
    steps = [("a", tuple(a_order[k : k + 2])) for k in range(0, per_dev, 2)]
    steps += [("b", (j,)) for j in b_order]
    n_tiles = 2 * per_dev + 3
    done, units, sent = [], [], set()
    for g, (kind, cells) in enumerate(steps):
        if kind == "a":
            continue
        done += cells
        ready = [
            t
            for t in range(n_tiles)
            if t not in sent
            and all(i in done for i in range(per_dev) if 2 * i <= t <= 2 * i + 4)
        ]
        sent.update(ready)
        runs = []
        for t in reversed(ready):
            if runs and runs[-1][0] == t + 1 and runs[-1][1] < 3:
                runs[-1] = (t, runs[-1][1] + 1)
            else:
                runs.append((t, 1))
        units += [(g, first, count) for first, count in runs]
    return steps, units


def kernel(
    per_dev,
    n_row,
    n_col,
    shifts_a,
    widths_a,
    shifts_b,
    widths_b,
    src_hbm,
    hbm_a,
    hbm_b,
    out,
    src,
    boxes,
    tgt,
    tgt_c,
    u_loc,
    mv_s,
    mv_u,
    canvas,
    band_hi,
    band_lo,
    r1,
    r2,
    rup,
    sb,
    cs,
    cl,
    s_send,
    s_recv,
    u_send,
    u_recv,
    x_send,
    x_recv,
    c_send,
    c_recv,
    b_sem,
):
    g = pl.program_id(0)
    cols = per_dev * S
    n_tiles = 2 * per_dev + 3
    row, col = lax.axis_index("row"), lax.axis_index("col")
    odd = lax.rem(row, 2) == 1
    even = lax.rem(row, 2) == 0
    steps, units = plan_of(per_dev)
    n_steps = len(steps)

    def pick(values):
        res = jnp.int32(values[0])
        for k in range(1, n_steps):
            res = jnp.where(g == k, jnp.int32(values[k]), res)
        return res

    j, j_c = pick([c[0] for _, c in steps]), pick([c[-1] for _, c in steps])
    is_a = pick([int(k == "a") for k, _ in steps]) == 1
    slots, held = [], []
    for kind, pair in steps:
        slots.append(range(len(held), len(held) + len(pair)))
        held += [(kind, i) for i in pair]
    slot, slot_c = pick([k[0] for k in slots]), pick([k[-1] for k in slots])

    def fetch(k):
        if k == len(held):
            return pltpu.make_async_copy(src_hbm, src, b_sem.at[k])
        kind, i = held[k]
        hbm = hbm_a if kind == "a" else hbm_b
        return pltpu.make_async_copy(hbm.at[0, i], boxes.at[k], b_sem.at[k])

    def at(dr, dc):
        return (lax.rem(row + dr + n_row, n_row), lax.rem(col + dc + n_col, n_col))

    def remote(a, b, send, recv, to):
        return pltpu.make_async_remote_copy(
            src_ref=a, dst_ref=b, send_sem=send, recv_sem=recv, device_id=to, device_id_type=MESH
        )

    upper, lower = slice(0, HALF), slice(HALF, S)
    edge = slice(cols - LANES, cols)

    def halo(field, moved, k, send, recv):
        if k == 0:
            a, b, to = field.at[upper, :LANES], moved.at[lower, edge], at(-1, -1)
        elif k == 1:
            a, b, to = field.at[lower, :LANES], moved.at[upper, edge], at(0, -1)
        else:
            lo, hi = max((k - 2) * S, HALF), (k - 1) * S
            a, b, to = field.at[upper, lo:hi], moved.at[lower, lo - HALF : hi - HALF], at(-1, 0)
        return remote(a, b, send.at[k], recv.at[k], to)

    def mass(k):
        return halo(src, mv_s, k, s_send, s_recv)

    def scale(k):
        return halo(u_loc, mv_u, k, u_send, u_recv)

    near, far = RADIUS + S, RADIUS + 2 * S
    mid = near + DOWN2

    def spill(n, kind):
        _, first, count = units[n]
        c = tiles(first, count)
        a, b, to, k = {
            "even_far": (canvas.at[far:, c], r1.at[S:, c], at(1, 0), 0),
            "even_near": (canvas.at[near:far, c], r1.at[:S, c], at(1, 0), 1),
            "odd_near": (canvas.at[near:mid, c], r1.at[:DOWN2, c], at(1, 0), 0),
            "odd_mid": (canvas.at[mid:far, c], r1.at[DOWN2:S, c], at(1, 0), 1),
            "odd_far": (canvas.at[far:, c], r2.at[:, c], at(2, 0), 2),
            "up": (canvas.at[:RADIUS, c], rup.at[:, c], at(-1, 0), 3),
        }[kind]
        return remote(a, b, x_send.at[n, k], x_recv.at[n, k], to)

    flank = slice(0, 3 * LANES)
    tip = slice(3 * LANES, 4 * LANES)

    def beside(k):
        if k == 0:
            a, b, to = sb.at[:, flank], cs.at[:, flank], at(0, 1)
        elif k == 1:
            a, b, to = sb.at[:, tip], cs.at[:, tip], at(0, 1)
        else:
            a, b, to = sb.at[:, tip], cl, at(0, -1)
        return remote(a, b, c_send.at[k], c_recv.at[k], to)

    sides = 2 if n_col == 2 else 3

    def give(n):
        @pl.when(even)
        def _():
            spill(n, "even_far").start()
            spill(n, "even_near").start()

        @pl.when(odd)
        def _():
            spill(n, "odd_far").start()
            spill(n, "odd_mid").start()

        spill(n, "up").start()

    def hand_on(n):
        @pl.when(odd)
        def _():
            c = tiles(units[n][1], units[n][2])
            spill(n, "even_far").wait_recv()
            canvas[near:mid, c] += r1[S:, c]
            spill(n, "odd_near").start()

    def between():
        for k in range(1, n_steps):
            ready = [n for n, u in enumerate(units) if u[0] == k - 1]
            if ready:

                @pl.when(g == k)
                def _():
                    for n in ready:
                        hand_on(n)

    def fold(n):
        c = tiles(units[n][1], units[n][2])

        @pl.when(even)
        def _():
            spill(n, "odd_near").wait_recv()
            spill(n, "odd_mid").wait_recv()
            canvas[OWN, c] += r1[:S, c]

        @pl.when(odd)
        def _():
            spill(n, "even_near").wait_recv()
            spill(n, "odd_far").wait_recv()
            canvas[OWN, c] += r1[:S, c]
            canvas[RADIUS : RADIUS + DOWN2, c] += r2[:, c]

        spill(n, "up").wait_recv()
        canvas[S : RADIUS + S, c] += rup[:, c]

    def smooth(first, count):
        lo, hi = max(first - 1, 0), min(first + count + 1, n_tiles)
        rows = slice((lo - first + 1) * LANES, (hi - first + 1) * LANES)
        field = split(canvas[OWN, lo * LANES : hi * LANES])
        return dot_split(field, [b[rows, : count * LANES] for b in (band_hi, band_lo)])

    def the_band():
        n = lax.broadcasted_iota(jnp.int32, (2 * S, S), 0)
        m = lax.broadcasted_iota(jnp.int32, (2 * S, S), 1)
        return split(blur_weight(n - LANES - m))

    @pl.when(is_a)
    def _():
        barrier = pltpu.get_barrier_semaphore()
        peers = [(-1, 0), (1, 0), (-2, 0), (2, 0), (0, -1), (0, 1), (-1, -1), (1, 1)]

        @pl.when(g == 0)
        def _():
            for dr, dc in peers:
                pl.semaphore_signal(barrier, inc=1, device_id=at(dr, dc), device_id_type=MESH)
            for k in slots[0]:
                fetch(k).start()
            fetch(len(held)).start()
            for k in range(slots[1][0], len(held)):
                fetch(k).start()
            canvas[...] = jnp.zeros_like(canvas)
            band_hi[...], band_lo[...] = the_band()

        cells = []
        for c in (j, j_c):
            o_r, o_c = shifts_a[0, 0, c], shifts_a[0, 1, c]
            krt, kc = gauss_t(o_r), gauss(o_c)
            in_r = bf(jnp.sum(krt.astype(jnp.float32), axis=1, keepdims=True)).astype(jnp.float32)
            in_c = jnp.sum(kc.astype(jnp.float32), axis=0, keepdims=True)
            cells.append((gauss(o_r), krt, kc, in_r * in_c))

        for n, (kind, _) in enumerate(steps):
            if kind == "a":

                @pl.when(g == n)
                def _():
                    for k in slots[n]:
                        fetch(k).wait()
                    if n == 0:
                        fetch(len(held)).wait()
                        mv_s[upper, : cols - HALF] = src[lower, HALF:]

        for n, (c, k, t) in enumerate(((j, slot, tgt), (j_c, slot_c, tgt_c))):
            t[...] = target_of(boxes[k], widths_a[0, 0, c], widths_a[0, 1, c])
            here = pl.ds(pl.multiple_of(c * S, S), S)
            kr, krt, kc, first = cells[n]
            cells[n] = (kr, krt, kc, t, src[:, here], here, first)
        back = [c[-1] for c in cells]
        for step in range(ITERS):
            v = [bf(c[3][...] / b) for c, b in zip(cells, back)]
            inner = [bf(dot(c[0], x)) for c, x in zip(cells, v)]
            u = [c[4] / dot_t(x, c[2]) for c, x in zip(cells, inner)]
            if step < ITERS - 1:
                inner = [bf(dot(c[1], bf(x))) for c, x in zip(cells, u)]
                back = [dot(x, c[2]) for c, x in zip(cells, inner)]
            if step == 0:

                @pl.when(g == 0)
                def _():
                    pl.semaphore_wait(barrier, len(peers))
                    for k in (0, 1, 1 + per_dev, 2):
                        mass(k).start()

        for c, x in zip(cells, u):
            u_loc[:, c[5]] = x

        for n, (kind, pair) in enumerate(steps):
            if kind == "b":
                continue

            @pl.when(g == n)
            def _():
                if n == 0:
                    scale(0).start()
                    scale(1).start()
                for i in reversed(pair):
                    scale(2 + i).start()
                if n == 0:
                    for k in range(per_dev, 2, -1):
                        mass(k).start()
                for i in pair:
                    lo, hi = max(i * S, HALF), (i + 1) * S
                    mv_u[upper, lo - HALF : hi - HALF] = u_loc[lower, lo:hi]

    @pl.when(jnp.logical_not(is_a))
    def _():
        waited = set()
        for k, (kind, pair) in enumerate(steps):
            if kind == "a":
                continue
            (i,) = pair
            need = [2 + c for c in (i, i + 1) if c < per_dev]
            need = [c for c in need + [0, 1] * (i == per_dev - 1) if c not in waited]
            waited.update(need)

            @pl.when(g == k)
            def _():
                fetch(slots[k][0]).wait()
                for c in need:
                    mass(c).wait_recv()
                    scale(c).wait_recv()

        o_r, o_c = shifts_b[0, 0, j], shifts_b[0, 1, j]
        h, w = widths_b[0, 0, j], widths_b[0, 1, j]
        kr = gauss(o_r)
        krt = gauss_t(o_r)
        kc = gauss(o_c)
        tgt[...] = target_of(boxes[slot], h, w)
        here = pl.ds(pl.multiple_of(j * S, S), S)
        a = mv_s[:, here]
        u = mv_u[:, here]
        for step in range(ITERS):
            back = dot(bf(dot(krt, bf(u))), kc)
            v = tgt[...] / back
            u = a / dot_t(bf(dot(kr, bf(v))), kc)
            if step == 0:
                between()

        plan = v * dot(bf(dot(krt, bf(u))), kc)

        r = lax.broadcasted_iota(jnp.int32, (LANES, 3 * LANES), 0) - RADIUS
        m = lax.broadcasted_iota(jnp.int32, (LANES, 3 * LANES), 1) - 2 * LANES
        weights = split(blur_weight(HALF + o_r + m - r))
        halves = split(plan)
        none = jnp.zeros((LANES, LANES), jnp.bfloat16)
        weights = [
            jnp.concatenate(
                [jnp.concatenate([x, none], axis=1), jnp.concatenate([none, x], axis=1)], axis=0
            )
            for x in weights
        ]
        parts = []
        for b in range(-(-TALL // S)):
            height = min(S, TALL - b * S)
            lo, hi = max(2 * b - 2, 0), min(2 * b + 2, BOX // LANES)
            wt = slice((lo - 2 * b + 2) * LANES, (hi - 2 * b + 2) * LANES)
            fine, rest = [x[:height, wt] for x in weights]
            top, low = [x[lo * LANES : hi * LANES] for x in halves]
            parts.append(dot_split((fine, rest), (top, low)))
        rowed = jnp.concatenate(parts, axis=0)
        s = HALF + o_c
        lane = lax.broadcasted_iota(jnp.int32, (TALL, LANES), 1)
        turned = [pltpu.roll(rowed[:, tiles(t, 1)], s, 1) for t in range(BOX // LANES)]
        zero = jnp.zeros((TALL, LANES), jnp.float32)
        for t in range(BOX // LANES + 1):
            left = turned[t - 1] if t > 0 else zero
            right = turned[t] if t < BOX // LANES else zero
            spot = pl.ds(pl.multiple_of(j * S + t * LANES, LANES), LANES)
            canvas[:, spot] += jnp.where(lane < s, left, right)

        for k in range(n_steps):
            ready = [n for n, u_ in enumerate(units) if u_[0] == k]
            if ready:

                @pl.when(g == k)
                def _():
                    for n in ready:
                        give(n)

        @pl.when(g == n_steps - 1)
        def _():
            final = [n for n, u_ in enumerate(units) if u_[0] == n_steps - 1]
            early = [n for n in range(len(units)) if n not in final]
            first = 2 * per_dev
            ready = set()

            def settle(need):
                while not need <= ready:
                    n = early.pop(0)
                    fold(n)
                    ready.update(range(units[n][1], units[n][1] + units[n][2]))

            settle({n_tiles - 1})
            for n in final:
                hand_on(n)
            settle(set(range(first - 1, n_tiles)))
            sb[:, 2 * LANES : 3 * LANES] = smooth(first + 2, 1)
            sb[:, : 2 * LANES] = smooth(first, 2)
            beside(0).start()
            settle({0})
            over = split(canvas[OWN, tiles(n_tiles - 1, 1)])
            under = split(canvas[OWN, tiles(0, 1)])
            sb[:, tip] = dot_split(over, [b[:LANES, :LANES] for b in (band_hi, band_lo)]) + dot_split(
                under, [b[2 * LANES : 3 * LANES, :LANES] for b in (band_hi, band_lo)]
            )
            for k in range(1, sides):
                beside(k).start()
            while early:
                settle({units[early[0]][1]})
            shown = set()

            def show():
                t = 2 * per_dev - 1
                while t >= 0:
                    ok = lambda x: x not in shown and all(
                        y in ready for y in (x - 1, x, x + 1) if 0 <= y < n_tiles
                    )
                    if ok(t):
                        count = 2 if t > 0 and ok(t - 1) else 1
                        base = t - count + 1
                        out[:, tiles(base, count)] = smooth(base, count)
                        shown.update(range(base, t + 1))
                        t -= count
                    else:
                        t -= 1

            show()
            for n in final:
                fold(n)
                ready.update(range(units[n][1], units[n][1] + units[n][2]))
                show()

            ln = lax.broadcasted_iota(jnp.int32, (S, LANES), 1)
            for k in range(sides):
                beside(k).wait_recv()
            out[:, flank] += cs[:, flank]
            out[:, tip] += jnp.where(ln < LANES - RADIUS, cs[:, tip], 0.0)
            behind = cs[:, tip] if n_col == 2 else cl[...]
            out[:, edge] += jnp.where(ln >= LANES - RADIUS, behind, 0.0)

            for k in range(2 + per_dev):
                mass(k).wait_send()
                scale(k).wait_send()
            for k in range(sides):
                beside(k).wait_send()
            for n in range(len(units)):
                spill(n, "up").wait_send()

                @pl.when(even)
                def _():
                    spill(n, "even_far").wait_send()
                    spill(n, "even_near").wait_send()

                @pl.when(odd)
                def _():
                    spill(n, "odd_near").wait_send()
                    spill(n, "odd_mid").wait_send()
                    spill(n, "odd_far").wait_send()


def on_device(n_row, n_col, source, boxes_a, shifts_a, widths_a, boxes_b, shifts_b, widths_b):
    cols = source.shape[1]
    per_dev = cols // S
    wide = cols + 3 * LANES
    steps, units = plan_of(per_dev)
    f32 = lambda *shape: pltpu.VMEM(shape, jnp.float32)
    dma = pltpu.SemaphoreType.DMA
    smem = pl.BlockSpec(memory_space=pltpu.SMEM)
    return pl.pallas_call(
        functools.partial(kernel, per_dev, n_row, n_col),
        grid_spec=pltpu.PrefetchScalarGridSpec(
            num_scalar_prefetch=0,
            grid=(len(steps),),
            in_specs=[
                smem,
                smem,
                smem,
                smem,
                *[pl.BlockSpec(memory_space=pl.ANY)] * 3,
            ],
            out_specs=pl.BlockSpec(memory_space=pltpu.VMEM),
            scratch_shapes=[
                f32(S, cols),
                f32(2 * per_dev, BOX, BOX),
                f32(BOX, BOX),
                f32(BOX, BOX),
                f32(S, cols),
                f32(S, cols),
                f32(S, cols),
                f32(TALL, wide),
                pltpu.VMEM((2 * S, S), jnp.bfloat16),
                pltpu.VMEM((2 * S, S), jnp.bfloat16),
                f32(S + DOWN2, wide),
                f32(DOWN2, wide),
                f32(RADIUS, wide),
                f32(S, 4 * LANES),
                f32(S, 4 * LANES),
                f32(S, LANES),
                dma((2 + per_dev,)),
                dma((2 + per_dev,)),
                dma((2 + per_dev,)),
                dma((2 + per_dev,)),
                dma((len(units), 4)),
                dma((len(units), 4)),
                dma((3,)),
                dma((3,)),
                dma((2 * per_dev + 1,)),
            ],
        ),
        out_shape=pltpu.VMEM((S, cols), jnp.float32),
        compiler_params=pltpu.CompilerParams(
            vmem_limit_bytes=56 * 1024 * 1024, collective_id=0, has_side_effects=True
        ),
        name="transport",
    )(*[x.swapaxes(1, 2) for x in (shifts_a, widths_a, shifts_b, widths_b)], source, boxes_a, boxes_b)


def solution(mesh):
    return jax.shard_map(
        functools.partial(on_device, mesh.shape["row"], mesh.shape["col"]),
        mesh=mesh,
        in_specs=(
            P("row", "col"),
            P("row", "col", None, None),
            P("row", "col", None),
            P("row", "col", None),
            P("row", "col", None, None),
            P("row", "col", None),
            P("row", "col", None),
        ),
        out_specs=P("row", "col"),
        check_vma=False,
    )
```
